512 devices in a mesh: dp: 128 (over z_lo, x, y, core), section: 4 (over z_hi).
Axes of the slice: x: 4, y: 4, z: 16 (z_hi: 4, z_lo: 4; z = z_hi * 4 + z_lo), core: 2. Of those that a mesh axis runs over, the one named last changes fastest.
Arguments:
- saved_inputs: bfloat16 [4, 2, 768, 6144], P('section', None, 'dp'), may hold values from -6 to 6
- carried: bfloat16 [4, 768, 6144], P('section', 'dp'), may hold values from -6 to 6
- head_grad: bfloat16 [768, 6144], P('dp'), may hold values from -6 to 6
- routing: int32 [4, 2, 768, 2], P('section', None, 'dp'), may hold values from 0 to 7, as said below
- replica_counts: int32 [128], replicated, may hold values from 2 to 5
- router: float32 [4, 6144, 8], P('section'), may hold values from -0.21875 to 0.21875
- w_in: bfloat16 [4, 128, 1536, 256], P('section', 'dp'), may hold values from -0.078125 to 0.078125
- w_out: bfloat16 [4, 128, 256, 1536], P('section', 'dp'), may hold values from -0.0625 to 0.0625
Outputs:
- input_grad: bfloat16 [2, 4, 768, 6144], P(None, 'section', 'dp')
- grad_in: bfloat16 [4, 128, 1536, 256], P('section', 'dp')
- grad_out: bfloat16 [4, 128, 256, 1536], P('section', 'dp')
- grad_router: float32 [4, 6144, 8], P('section')
The draws below stay inside these ranges and needn't reach their ends.
Inputs may be any that keep to these rules, and one draw needn't show every extreme that they name: `routing`: each row names 2 different experts; in every section and step at most 2 of one device's 6 tokens name expert 0, and exactly 2 on some device.
All inputs are finite; a program needn't handle non-finite values.
Results may differ from the reference program's by a relative error of at most 0.0057.
Values may be sent and summed in bfloat16 or wider, within the bound.
A program may use at most 64 MiB of HBM per device.

```python
import jax
import jax.numpy as jnp
from jax import lax

D = 6144
FF = 8192
EXPERTS = 8
TOP = 2
STEPS = 2
CAP = 2
TOK_DEV = 6
SECTIONS = 4
TOKENS = 768
GROUPS = 32
D_PART = 1536
HID_DEV = 256
ROWS = 256
N_DP = 128


def draw_routing(key, part):
    keys = jax.random.split(key, 5)
    shape = (SECTIONS, STEPS, N_DP, TOK_DEV)
    base = jax.random.randint(keys[0], shape, 1, EXPERTS, dtype=jnp.int32)
    offset = jax.random.randint(keys[1], shape, 1, EXPERTS - 1, dtype=jnp.int32)
    second = 1 + (base - 1 + offset) % (EXPERTS - 1)
    count = jax.random.randint(keys[2], (SECTIONS, STEPS, N_DP), CAP // 2 + 1, CAP + 1, dtype=jnp.int32)
    fullest = jax.random.randint(keys[3], (SECTIONS, STEPS, 1), 0, N_DP, dtype=jnp.int32)
    count = jnp.where(jnp.arange(N_DP, dtype=jnp.int32)[None, None, :] == fullest, CAP, count)
    scores = jax.random.randint(keys[4], shape, 0, 1 << 20, dtype=jnp.int32) * TOK_DEV + jnp.arange(TOK_DEV, dtype=jnp.int32)
    order = jnp.argsort(scores, axis=3, stable=True)
    ranks = jnp.argsort(order, axis=3, stable=True).astype(jnp.int32)
    first = jnp.where(ranks < count[..., None], 0, base)
    return jnp.stack([first, second], axis=-1).reshape(SECTIONS, STEPS, TOKENS, TOP).astype(jnp.int32)


def touch_ends(result, key, low, largest):
    place = [jax.random.randint(jax.random.fold_in(key, axis), (), 0, length) for axis, length in enumerate(result.shape)]
    widest = result.shape.index(max(result.shape))
    beside = place[:widest] + [(place[widest] + 1) % result.shape[widest]] + place[widest + 1:]
    return result.at[tuple(place)].set(low).at[tuple(beside)].set(largest)


def block_levels(key, shape, cuts, low, largest):
    level, own = 1.0, jax.random.fold_in(key, 6)
    for axis_at, parts in cuts:
        heights = jnp.exp(jax.random.uniform(jax.random.fold_in(own, axis_at), (parts,), jnp.float32, low / len(cuts), largest / len(cuts)))
        level = level * jnp.repeat(heights, shape[axis_at] // parts).reshape([-1 if axis == axis_at else 1 for axis in range(len(shape))])
    return level


def noise(rng, shape, spread, most, shards=(), kind=jnp.bfloat16):
    values = jax.random.normal(rng, shape, jnp.float32) * spread
    if len(shards) > 0:
        values = block_levels(rng, shape, shards, -0.22, 0.18) * values
    return jnp.clip(values, min=-most, max=most).astype(kind)


def setup_inputs(seed: int = 0) -> dict:
    arg_keys = jax.random.split(jax.random.key(seed), 9)
    saved_inputs = noise(arg_keys[0], (SECTIONS, STEPS, TOKENS, D), 1.0, 6.0, ((0, 4), (2, 128)))
    carried = noise(arg_keys[1], (SECTIONS, TOKENS, D), 1.0, 6.0, ((0, 4), (1, 128)))
    head_grad = noise(arg_keys[2], (TOKENS, D), 1.0, 6.0, ((0, 128),))
    routing = draw_routing(jax.random.fold_in(arg_keys[8], 71), 0)
    replica_counts = touch_ends(jax.random.randint(arg_keys[4], (N_DP,), 2, SECTIONS + 2), jax.random.fold_in(arg_keys[4], 1), 2, (SECTIONS + 2) - 1).astype(jnp.int32)
    router = noise(arg_keys[5], (SECTIONS, D, EXPERTS), (D // 9) ** -0.5, 0.21875, ((0, 4),), jnp.float32)
    w_in = noise(arg_keys[6], (SECTIONS, N_DP, D_PART, HID_DEV), D ** -0.5, 0.078125, ((0, 4), (1, 128)))
    w_out = noise(arg_keys[7], (SECTIONS, N_DP, HID_DEV, D_PART), FF ** -0.5, 0.0625, ((0, 4), (1, 128)))
    return {"saved_inputs": saved_inputs, "carried": carried, "head_grad": head_grad, "routing": routing, "replica_counts": replica_counts, "router": router, "w_in": w_in, "w_out": w_out}


def silu_grad(value):
    sig = jax.nn.sigmoid(value)
    return sig * (1.0 + value * (1.0 - sig))

def full_in(block):
    return block.reshape(GROUPS, 4, D_PART, HID_DEV).transpose(1, 2, 0, 3).reshape(D, FF)

def block_in(full):
    return full.reshape(4, D_PART, GROUPS, HID_DEV).transpose(2, 0, 1, 3).reshape(N_DP, D_PART, HID_DEV)

def full_out(block):
    return block.reshape(GROUPS, 4, HID_DEV, D_PART).transpose(0, 2, 1, 3).reshape(FF, D)

def block_out(full):
    return full.reshape(GROUPS, HID_DEV, 4, D_PART).transpose(0, 2, 1, 3).reshape(N_DP, HID_DEV, D_PART)

def slot_table(ids, live_tok):
    routed = ((ids[:, 0] == 0) | (ids[:, 1] == 0)) & live_tok
    flags = routed.reshape(N_DP, TOK_DEV).astype(jnp.int32)
    slot = jnp.cumsum(flags, axis=1, dtype=jnp.int32) - 1
    slots = jnp.arange(CAP, dtype=jnp.int32)
    table = (slot[:, None, :] == slots[None, :, None]) & (flags[:, None, :] == 1)
    return table.astype(jnp.float32)

def section_back(xin, incoming, ids, live_rep, router_w, weight_in, weight_out):
    hi = lax.Precision.HIGHEST
    live_tok = jnp.repeat(live_rep, TOK_DEV)
    dy = jnp.where(live_tok[:, None], incoming, jnp.zeros_like(incoming))
    xf = xin.astype(jnp.float32)
    logits = jnp.dot(xf, router_w, precision=hi)
    expo = jnp.exp(logits)
    prob = expo / lax.optimization_barrier(jnp.sum(expo, axis=1, keepdims=True))
    table = slot_table(ids, live_tok)
    xs = jnp.einsum('jct,jtd->jcd', table, xf.reshape(N_DP, TOK_DEV, D), precision=hi).reshape(ROWS, D).astype(jnp.bfloat16)
    ys = jnp.einsum('jct,jtd->jcd', table, dy.astype(jnp.float32).reshape(N_DP, TOK_DEV, D), precision=hi).reshape(ROWS, D).astype(jnp.bfloat16)
    gate = jnp.einsum('jct,jt->jc', table, prob[:, 0].reshape(N_DP, TOK_DEV), precision=hi).reshape(ROWS).astype(jnp.bfloat16)
    pre = jnp.dot(xs, weight_in, preferred_element_type=jnp.float32)
    upper = lax.dot_general(ys, weight_out, (((1,), (1,)), ((), ())), preferred_element_type=jnp.float32)
    act = jax.nn.silu(pre)
    gate_f = gate.astype(jnp.float32)[:, None]
    dpre = (gate_f * upper * silu_grad(pre)).astype(jnp.bfloat16)
    scaled = (gate_f * act).astype(jnp.bfloat16)
    block_sums = lax.optimization_barrier(jnp.sum((act * upper).reshape(ROWS, GROUPS, HID_DEV), axis=2))
    block_sums = lax.optimization_barrier(block_sums.astype(jnp.bfloat16)).astype(jnp.float32)
    dgate = lax.optimization_barrier(jnp.sum(block_sums, axis=1))

    def group_term(total, group):
        piece = lax.dynamic_slice_in_dim(dpre, group * HID_DEV, HID_DEV, 1)
        wpiece = lax.dynamic_slice_in_dim(weight_in, group * HID_DEV, HID_DEV, 1)
        term = lax.dot_general(piece, wpiece, (((1,), (1,)), ((), ())), preferred_element_type=jnp.float32)
        term = lax.optimization_barrier(term.astype(jnp.bfloat16)).astype(jnp.float32)
        return (total + term, None)
    dxs, _ = lax.scan(group_term, jnp.zeros((ROWS, D), jnp.float32), jnp.arange(GROUPS, dtype=jnp.int32))
    grad_one = lax.dot_general(xs, dpre, (((0,), (0,)), ((), ())), preferred_element_type=jnp.float32)
    grad_two = lax.dot_general(scaled, ys, (((0,), (0,)), ((), ())), preferred_element_type=jnp.float32)
    dxe = jnp.einsum('jct,jcd->jtd', table, dxs.reshape(N_DP, CAP, D), precision=hi).reshape(TOKENS, D)
    dg_tok = jnp.einsum('jct,jc->jt', table, dgate.reshape(N_DP, CAP), precision=hi).reshape(TOKENS)
    first = (jnp.arange(EXPERTS, dtype=jnp.int32) == 0).astype(jnp.float32)
    dlog = (dg_tok * prob[:, 0])[:, None] * (first[None, :] - prob)
    dx = dy.astype(jnp.float32) + dxe + jnp.dot(dlog, router_w.T, precision=hi)
    grad_r = jnp.dot(xf.T, dlog, precision=hi)
    return (dx.astype(jnp.bfloat16), grad_one, grad_two, grad_r)

def reference(saved_inputs, carried, head_grad, routing, replica_counts, router, w_in, w_out):
    first_dx = []
    totals = []
    for section in range(SECTIONS):
        weight_in = full_in(w_in[section])
        weight_out = full_out(w_out[section])
        live_rep = section < replica_counts
        out = section_back(saved_inputs[section, 0], carried[section], routing[section, 0], live_rep, router[section], weight_in, weight_out)
        first_dx.append(out[0])
        totals.append(out[1:])
    second_dx = [None] * SECTIONS
    grads_in = [None] * SECTIONS
    grads_out = [None] * SECTIONS
    grads_r = [None] * SECTIONS
    for section in range(SECTIONS - 1, -1, -1):
        weight_in = full_in(w_in[section])
        weight_out = full_out(w_out[section])
        incoming = head_grad if section == SECTIONS - 1 else first_dx[section + 1]
        live_rep = section + 1 < replica_counts
        out = section_back(saved_inputs[section, 1], incoming, routing[section, 1], live_rep, router[section], weight_in, weight_out)
        second_dx[section] = out[0]
        grads_in[section] = block_in((totals[section][0] + out[1]).astype(jnp.bfloat16))
        grads_out[section] = block_out((totals[section][1] + out[2]).astype(jnp.bfloat16))
        grads_r[section] = totals[section][2] + out[3]
    input_grad = jnp.stack([jnp.stack(first_dx), jnp.stack(second_dx)])
    return (input_grad, jnp.stack(grads_in), jnp.stack(grads_out), jnp.stack(grads_r))
```

```python
import functools

import jax
import jax.numpy as jnp
from jax import lax
from jax.experimental import pallas as pl
from jax.experimental.pallas import tpu as pltpu
from jax.sharding import PartitionSpec as P

STEPS = 2
CAP = 2
EXT = 128


def shifted(array, axis, by):
    devices = lax.axis_size(axis)
    pairs = [(i, i + by) for i in range(devices) if 0 <= i + by < devices]
    return lax.ppermute(array, axis, pairs)


def rounded(value):
    return value.astype(jnp.bfloat16).astype(jnp.float32)


def split_ext(value):
    lanes = lax.broadcasted_iota(jnp.int32, value.shape[:-1] + (EXT,), len(value.shape) - 1)
    high = rounded(value)
    return jnp.where(lanes < EXT // 2, high, value - high)


def step_kernel(first_step, part, hidden, *refs):
    if first_step:
        (pay, w_in, w_out, back, gin, gout, xq, near, rows, pu, ra, sb, rb, dd,
         dx, rx, dz, rz, fin, split, rf, send, recv, own) = refs
        acc_in = acc_out = None
    else:
        (pay, w_in, w_out, acc_in, acc_out, back, gin, gout, xq, near, rows, pu, ra, sb, rb, dd,
         dx, rx, dz, rz, fin, split, rf, send, recv, own) = refs
    wide = part + EXT
    f32 = jnp.float32
    me = lax.axis_index("dp")
    line = me % 8
    base = me - line
    core = me % 2
    odd = (me // 2) % 2
    xpos = (me // 8) % 4
    zpos = me // 32

    def near_dev(r):
        return base + (line + r) % 8

    def z_dev(r):
        return ((zpos + r) % 4) * 32 + xpos * 8 + line

    def x_dev(r):
        return zpos * 32 + ((xpos + r) % 4) * 8 + line

    core_dev = base + (line // 2) * 2 + (1 - core)
    odd_dev = base + (line // 4) * 4 + (1 - odd) * 2 + core

    barrier = pltpu.get_barrier_semaphore()
    peers = [near_dev(r) for r in range(1, 8)]
    peers += [z_dev(r) for r in range(1, 4)] + [x_dev(r) for r in range(1, 4)]
    for peer in peers:
        pl.semaphore_signal(barrier, inc=1, device_id={"dp": peer}, device_id_type=pl.DeviceIdType.MESH)
    pl.semaphore_wait(barrier, len(peers))

    def copy(src, dst, slot, device):
        return pltpu.make_async_remote_copy(
            src_ref=src, dst_ref=dst, send_sem=send.at[slot], recv_sem=recv.at[slot],
            device_id={"dp": device}, device_id_type=pl.DeviceIdType.MESH)

    mine = pltpu.make_async_copy(pay.at[line % 4], near.at[line], own.at[0])
    mine.start()
    sent = []
    for r in range(1, 8):
        c = copy(pay.at[(line + r) % 4], near.at[line], r - 1, near_dev(r))
        c.start()
        sent.append(c)
    mine.wait()
    for r in range(1, 8):
        copy(pay.at[0], near.at[(line + 8 - r) % 8], r - 1, near_dev(r)).wait_recv()
    total = 2 * part + EXT
    chunk = 640
    for at in range(0, total, chunk):
        index = lax.broadcasted_iota(jnp.int32, (16, chunk), 0)
        block = jnp.zeros((16, chunk), f32)
        for s in range(8):
            pair = near[s, :, at:at + chunk].astype(f32)
            for k in range(2):
                block = jnp.where(index == 2 * s + k, pair[k:k + 1], block)
        rows[zpos, xpos, :, at:at + chunk] = block.astype(jnp.bfloat16)
    for r in range(1, 4):
        c = copy(rows.at[zpos, xpos], rows.at[zpos, xpos], 6 + r, z_dev(r))
        c.start()
        sent.append(c)
    for r in range(1, 4):
        copy(rows.at[zpos, xpos], rows.at[(zpos + 4 - r) % 4, xpos], 6 + r, z_dev(r)).wait_recv()
    for r in range(1, 4):
        c = copy(rows.at[:, xpos], rows.at[:, xpos], 9 + r, x_dev(r))
        c.start()
        sent.append(c)
    for r in range(1, 4):
        copy(rows.at[:, xpos], rows.at[:, (xpos + 4 - r) % 4], 9 + r, x_dev(r)).wait_recv()

    def matrix(low, high):
        return rows[:, :, :, low:high].reshape(256, high - low)

    pre = jnp.dot(matrix(0, part), w_in[...], preferred_element_type=f32)
    pu[:, :, 0:hidden] = pre.reshape(4, 64, hidden)
    upper = lax.dot_general(matrix(part, 2 * part), w_out[...], (((1,), (1,)), ((), ())), preferred_element_type=f32)
    pu[:, :, hidden:2 * hidden] = upper.reshape(4, 64, hidden)

    c = copy(pu.at[pl.ds(2 * (1 - core), 2)], ra, 13, core_dev)
    c.start()
    sent.append(c)
    c.wait_recv()
    sb[...] = pu[pl.ds(2 * core, 2)] + ra[...]
    c = copy(sb.at[1 - odd], rb, 14, odd_dev)
    c.start()
    sent.append(c)
    c.wait_recv()
    k = 2 * core + odd
    both = sb[odd] + rb[...]
    pre = both[:, 0:hidden]
    upper = both[:, hidden:2 * hidden]
    gate = rows[k, :, :, 2 * part:2 * part + EXT].reshape(64, EXT).astype(f32)[:, 0:1]
    sig = jax.nn.sigmoid(pre)
    act = pre * sig
    dd[k, :, 0:hidden] = (gate * upper * (sig * (1.0 + pre * (1.0 - sig)))).astype(jnp.bfloat16)
    dd[k, :, hidden:2 * hidden] = (gate * act).astype(jnp.bfloat16)
    sums = jnp.sum(act * upper, axis=1, keepdims=True)
    dd[k, :, 2 * hidden:2 * hidden + EXT] = jnp.broadcast_to(sums, (64, EXT)).astype(jnp.bfloat16)
    c = copy(dd.at[k], dd.at[k], 15, odd_dev)
    c.start()
    sent.append(c)
    copy(dd.at[k], dd.at[2 * core + 1 - odd], 15, odd_dev).wait_recv()
    c = copy(dd.at[pl.ds(2 * core, 2)], dd.at[pl.ds(2 * core, 2)], 16, core_dev)
    c.start()
    sent.append(c)
    copy(dd.at[pl.ds(2 * core, 2)], dd.at[pl.ds(2 * (1 - core), 2)], 16, core_dev).wait_recv()

    dpre = dd[:, :, 0:hidden].reshape(256, hidden)
    scaled = dd[:, :, hidden:2 * hidden].reshape(256, hidden)
    term = lax.dot_general(dpre, w_in[...], (((1,), (1,)), ((), ())), preferred_element_type=f32)
    dx[:, :, :, 0:part] = term.astype(jnp.bfloat16).reshape(4, 4, 16, part)
    sums = dd[:, :, 2 * hidden:2 * hidden + EXT].reshape(256, EXT).astype(f32)
    lanes = lax.broadcasted_iota(jnp.int32, (256, EXT), 1)
    sums = jnp.where(lanes < EXT // 2, sums, 0.0)
    dx[:, :, :, part:wide] = sums.astype(jnp.bfloat16).reshape(4, 4, 16, EXT)
    for r in range(1, 4):
        c = copy(dx.at[:, (xpos + r) % 4], rx.at[r - 1], 16 + r, x_dev(r))
        c.start()
        sent.append(c)
    one = lax.dot_general(matrix(0, part), dpre, (((0,), (0,)), ((), ())), preferred_element_type=f32)
    two = lax.dot_general(scaled, matrix(part, 2 * part), (((0,), (0,)), ((), ())), preferred_element_type=f32)
    if first_step:
        gin[...] = one
        gout[...] = two
    else:
        gin[...] = (acc_in[...] + one).astype(jnp.bfloat16)
        gout[...] = (acc_out[...] + two).astype(jnp.bfloat16)
    xq[...] = matrix(0, part)
    for r in range(1, 4):
        copy(dx.at[:, 0], rx.at[r - 1], 16 + r, x_dev(r)).wait_recv()
    for z in range(4):
        value = dx[z, xpos].astype(f32)
        for r in range(3):
            value = value + rx[r, z].astype(f32)
        dz[z, :, 0:part] = value[:, 0:part].astype(jnp.bfloat16)
        column = value[:, part:part + 1] + value[:, part + EXT // 2:part + EXT // 2 + 1]
        dz[z, :, part:wide] = split_ext(column).astype(jnp.bfloat16)
    for r in range(1, 4):
        c = copy(dz.at[(zpos + r) % 4], rz.at[r - 1], 19 + r, z_dev(r))
        c.start()
        sent.append(c)
    for r in range(1, 4):
        copy(dz.at[0], rz.at[r - 1], 19 + r, z_dev(r)).wait_recv()
    value = dz[zpos].astype(f32)
    for r in range(3):
        value = value + rz[r].astype(f32)
    fin[:, 0:part] = value[:, 0:part]
    column = value[:, part:part + 1] + value[:, part + EXT // 2:part + EXT // 2 + 1]
    fin[:, part:wide] = jnp.broadcast_to(column, (16, EXT))
    for s in range(8):
        split[s] = fin[2 * s:2 * s + 2, :]
    mine = pltpu.make_async_copy(split.at[line], rf.at[line], own.at[1])
    mine.start()
    for r in range(1, 8):
        c = copy(split.at[(line + r) % 8], rf.at[line], 22 + r, near_dev(r))
        c.start()
        sent.append(c)
    mine.wait()
    for r in range(1, 8):
        copy(split.at[0], rf.at[(line + 8 - r) % 8], 22 + r, near_dev(r)).wait_recv()
    back[...] = rf[0:4] + rf[4:8]
    for c in sent:
        c.wait_send()


def run_step(first_step, payload, w_in, w_out, *acc):
    part, hidden = w_in.shape
    wide = part + EXT
    total = 2 * part + EXT
    bf16, f32 = jnp.bfloat16, jnp.float32
    grad = f32 if first_step else bf16
    vmem = pl.BlockSpec(memory_space=pltpu.VMEM)
    copies = 30
    return pl.pallas_call(
        functools.partial(step_kernel, first_step, part, hidden),
        out_shape=(
            jax.ShapeDtypeStruct((4, CAP, wide), f32),
            jax.ShapeDtypeStruct((part, hidden), grad),
            jax.ShapeDtypeStruct((hidden, part), grad),
            jax.ShapeDtypeStruct((256, part), bf16),
        ),
        in_specs=[vmem] * (3 + len(acc)),
        out_specs=(vmem,) * 4,
        scratch_shapes=[
            pltpu.VMEM((8, CAP, total), bf16),
            pltpu.VMEM((4, 4, 16, total), bf16),
            pltpu.VMEM((4, 64, 2 * hidden), f32),
            pltpu.VMEM((2, 64, 2 * hidden), f32),
            pltpu.VMEM((2, 64, 2 * hidden), f32),
            pltpu.VMEM((64, 2 * hidden), f32),
            pltpu.VMEM((4, 64, 2 * hidden + EXT), bf16),
            pltpu.VMEM((4, 4, 16, wide), bf16),
            pltpu.VMEM((3, 4, 16, wide), bf16),
            pltpu.VMEM((4, 16, wide), bf16),
            pltpu.VMEM((3, 16, wide), bf16),
            pltpu.VMEM((16, wide), f32),
            pltpu.VMEM((8, CAP, wide), f32),
            pltpu.VMEM((8, CAP, wide), f32),
            pltpu.SemaphoreType.DMA((copies,)),
            pltpu.SemaphoreType.DMA((copies,)),
            pltpu.SemaphoreType.DMA((2,)),
        ],
        compiler_params=pltpu.CompilerParams(
            collective_id=0 if first_step else 1, has_side_effects=True, vmem_limit_bytes=48 << 20
        ),
    )(payload, w_in, w_out, *acc)


def router_kernel(experts, pay, x0, x1, out, near, every, mine, parts, send, recv, own):
    f32 = jnp.float32
    me = lax.axis_index("dp")
    line = me % 8
    base = me - line
    quarter = me % 4
    xpos = (me // 8) % 4
    zpos = me // 32

    def near_dev(r):
        return base + (line + r) % 8

    def z_dev(r):
        return ((zpos + r) % 4) * 32 + xpos * 8 + line

    def x_dev(r):
        return zpos * 32 + ((xpos + r) % 4) * 8 + line

    def quarter_dev(r):
        return base + (line // 4) * 4 + (quarter + r) % 4

    barrier = pltpu.get_barrier_semaphore()
    peers = [near_dev(r) for r in range(1, 8)]
    peers += [z_dev(r) for r in range(1, 4)] + [x_dev(r) for r in range(1, 4)]
    for peer in peers:
        pl.semaphore_signal(barrier, inc=1, device_id={"dp": peer}, device_id_type=pl.DeviceIdType.MESH)
    pl.semaphore_wait(barrier, len(peers))

    def copy(src, dst, slot, device):
        return pltpu.make_async_remote_copy(
            src_ref=src, dst_ref=dst, send_sem=send.at[slot], recv_sem=recv.at[slot],
            device_id={"dp": device}, device_id_type=pl.DeviceIdType.MESH)

    sent = []
    local_copy = pltpu.make_async_copy(pay, near.at[line], own.at[0])
    local_copy.start()
    for r in range(1, 8):
        c = copy(pay, near.at[line], r - 1, near_dev(r))
        c.start()
        sent.append(c)
    local_copy.wait()
    for r in range(1, 8):
        copy(pay, near.at[(line + 8 - r) % 8], r - 1, near_dev(r)).wait_recv()
    index = lax.broadcasted_iota(jnp.int32, (16, 128), 0)
    for step in range(2):
        block = jnp.zeros((16, 128), f32)
        for s in range(8):
            four = near[s]
            for k in range(2):
                block = jnp.where(index == 2 * s + k, four[2 * step + k:2 * step + k + 1], block)
        every[zpos, xpos, step] = block.astype(jnp.bfloat16)
    for r in range(1, 4):
        c = copy(every.at[zpos, xpos], every.at[zpos, xpos], 6 + r, z_dev(r))
        c.start()
        sent.append(c)
    for r in range(1, 4):
        copy(every.at[zpos, xpos], every.at[(zpos + 4 - r) % 4, xpos], 6 + r, z_dev(r)).wait_recv()
    for r in range(1, 4):
        c = copy(every.at[:, xpos], every.at[:, xpos], 9 + r, x_dev(r))
        c.start()
        sent.append(c)
    for r in range(1, 4):
        copy(every.at[:, xpos], every.at[:, (xpos + 4 - r) % 4], 9 + r, x_dev(r)).wait_recv()
    total = None
    for step, x in enumerate((x0, x1)):
        term = lax.dot_general(every[:, :, step].reshape(256, 128), x[...], (((0,), (0,)), ((), ())),
                               preferred_element_type=f32)
        total = term if total is None else total + term
    mine[...] = total[0:experts] + total[experts:2 * experts] + total[2 * experts:3 * experts]
    local_copy = pltpu.make_async_copy(mine, parts.at[quarter], own.at[1])
    local_copy.start()
    for r in range(1, 4):
        c = copy(mine, parts.at[quarter], 12 + r, quarter_dev(r))
        c.start()
        sent.append(c)
    local_copy.wait()
    for r in range(1, 4):
        copy(mine, parts.at[(quarter + 4 - r) % 4], 12 + r, quarter_dev(r)).wait_recv()
    out[...] = parts[...]
    for c in sent:
        c.wait_send()


def run_router(experts, lanes, x0, x1):
    part = x0.shape[1]
    f32 = jnp.float32
    vmem = pl.BlockSpec(memory_space=pltpu.VMEM)
    return pl.pallas_call(
        functools.partial(router_kernel, experts),
        out_shape=jax.ShapeDtypeStruct((4, experts, part), f32),
        in_specs=[vmem] * 3,
        out_specs=vmem,
        scratch_shapes=[
            pltpu.VMEM((8, 8, 128), f32),
            pltpu.VMEM((4, 4, 2, 16, 128), jnp.bfloat16),
            pltpu.VMEM((experts, part), f32),
            pltpu.VMEM((4, experts, part), f32),
            pltpu.SemaphoreType.DMA((16,)),
            pltpu.SemaphoreType.DMA((16,)),
            pltpu.SemaphoreType.DMA((2,)),
        ],
        compiler_params=pltpu.CompilerParams(
            collective_id=2, has_side_effects=True, vmem_limit_bytes=48 << 20
        ),
    )(lanes, x0, x1)


def dlog_slots(table, dlog):
    return jnp.dot(table, dlog, precision=lax.Precision.HIGHEST)


def local(saved_inputs, carried, head_grad, routing, replica_counts, router, w_in, w_out):
    hi = lax.Precision.HIGHEST
    section_count = lax.axis_size("section")
    section_index = lax.axis_index("section")
    dev_index = lax.axis_index("dp")
    width = head_grad.shape[1]
    part = w_in.shape[2]
    experts = router.shape[2]
    router_w = router[0]
    my_count = replica_counts[dev_index]
    first = (jnp.arange(experts) == 0).astype(jnp.float32)
    slots = jnp.arange(CAP, dtype=jnp.int32)

    def prepare(step):
        xin = saved_inputs[0, step]
        ids = routing[0, step]
        live = step + section_index < my_count
        xf = xin.astype(jnp.float32)
        logits = jnp.dot(xf, router_w, precision=hi)
        expo = jnp.exp(logits)
        prob = expo / jnp.sum(expo, axis=1, keepdims=True)
        routed = ((ids[:, 0] == 0) | (ids[:, 1] == 0)) & live
        slot = jnp.cumsum(routed.astype(jnp.int32), dtype=jnp.int32) - 1
        table = ((slot[None, :] == slots[:, None]) & routed[None, :]).astype(jnp.float32)
        xs = jnp.dot(table.astype(jnp.bfloat16), xin, preferred_element_type=jnp.float32).astype(jnp.bfloat16)
        gate = jnp.dot(table, prob[:, 0], precision=hi).astype(jnp.bfloat16)
        return (xf, prob, table, live, xs, gate)

    def quarters(rows):
        return rows.reshape(CAP, 4, part).transpose(1, 0, 2)

    prepared = [prepare(step) for step in range(STEPS)]
    outputs, logs, inputs = [], [], []
    incoming = carried[0]
    acc = ()
    for step in range(STEPS):
        xf, prob, table, live, xs, gate = prepared[step]
        if step == 1:
            passed = shifted(outputs[0], "section", -1)
            incoming = jnp.where(section_index == section_count - 1, head_grad, passed)
        grad_in_tok = jnp.where(live, incoming, jnp.zeros_like(incoming))
        ys = jnp.dot(table.astype(jnp.bfloat16), grad_in_tok, preferred_element_type=jnp.float32).astype(jnp.bfloat16)
        payload = jnp.concatenate(
            [quarters(xs), quarters(ys), jnp.broadcast_to(gate[None, :, None], (4, CAP, EXT))], axis=2)
        back, *acc, xq = run_step(step == 0, payload, w_in[0, 0], w_out[0, 0], *acc)
        dxs = back[:, :, :part].transpose(1, 0, 2).reshape(CAP, width)
        dgate = back[0, :, part]
        dxe = lax.dot_general(table, dxs, (((0,), (0,)), ((), ())), precision=hi)
        dg_tok = lax.dot_general(table, dgate, (((0,), (0,)), ((), ())), precision=hi)
        dlog = (dg_tok * prob[:, 0])[:, None] * (first[None, :] - prob)
        result = grad_in_tok.astype(jnp.float32) + dxe + jnp.dot(dlog, router_w.T, precision=hi)
        outputs.append(result.astype(jnp.bfloat16))
        logs.append(dlog_slots(table, dlog))
        inputs.append(xq)
    lanes = jnp.concatenate(logs)
    high = rounded(lanes)
    middle = rounded(lanes - high)
    low = lanes - high - middle
    lanes = jnp.concatenate([high, middle, low], axis=1)
    lanes = jnp.pad(lanes, ((0, 8 - lanes.shape[0]), (0, 128 - lanes.shape[1])))
    grad_router = run_router(experts, lanes, *inputs).transpose(0, 2, 1).reshape(width, experts)
    return (jnp.stack(outputs)[:, None], acc[0][None, None], acc[1][None, None], grad_router[None])


def solution(mesh):
    in_specs = (
        P("section", None, "dp", None),
        P("section", "dp", None),
        P("dp", None),
        P("section", None, "dp", None),
        P(),
        P("section", None, None),
        P("section", "dp", None, None),
        P("section", "dp", None, None),
    )
    out_specs = (
        P(None, "section", "dp", None),
        P("section", "dp", None, None),
        P("section", "dp", None, None),
        P("section", None, None),
    )
    return jax.shard_map(local, mesh=mesh, in_specs=in_specs, out_specs=out_specs, check_vma=False)
```

```python
import functools

import jax
import jax.numpy as jnp
from jax import lax
from jax.experimental import pallas as pl
from jax.experimental.pallas import tpu as pltpu
from jax.sharding import PartitionSpec as P

STEPS = 2
CAP = 2
EXT = 128


def shifted(array, axis, by):
    devices = lax.axis_size(axis)
    pairs = [(i, i + by) for i in range(devices) if 0 <= i + by < devices]
    return lax.ppermute(array, axis, pairs)


def rounded(value):
    return value.astype(jnp.bfloat16).astype(jnp.float32)


def split_ext(value):
    lanes = lax.broadcasted_iota(jnp.int32, value.shape[:-1] + (EXT,), len(value.shape) - 1)
    high = rounded(value)
    return jnp.where(lanes < EXT // 2, high, value - high)


def step_kernel(first_step, part, hidden, experts, names, *refs):
    ref = dict(zip(names, refs))
    pay_y, w_in, w_out = ref["pay_y"], ref["w_in"], ref["w_out"]
    send, recv, own = ref["send"], ref["recv"], ref["own"]
    wide = part + EXT
    f32, bf16 = jnp.float32, jnp.bfloat16
    me = lax.axis_index("dp")
    line = me % 8
    base = me - line
    core = me % 2
    odd = (me // 2) % 2
    half = line // 4
    quarter = me % 4
    xpos = (me // 8) % 4
    zpos = me // 32
    ahead, behind, across = (xpos + 1) % 4, (xpos + 3) % 4, (xpos + 2) % 4

    def near_dev(r):
        return base + (line + r) % 8

    def z_dev(r):
        return ((zpos + r) % 4) * 32 + xpos * 8 + line

    def x_dev(r):
        return zpos * 32 + ((xpos + r) % 4) * 8 + line

    core_dev = base + (line // 2) * 2 + (1 - core)
    odd_dev = base + half * 4 + (1 - odd) * 2 + core
    half_dev = base + (line + 4) % 8

    barrier = pltpu.get_barrier_semaphore()
    peers = [near_dev(r) for r in range(1, 8)]
    peers += [z_dev(r) for r in range(1, 4)] + [x_dev(r) for r in range(1, 4)]
    for peer in peers:
        pl.semaphore_signal(barrier, inc=1, device_id={"dp": peer}, device_id_type=pl.DeviceIdType.MESH)
    pl.semaphore_wait(barrier, len(peers))

    def copy(src, dst, slot, device):
        return pltpu.make_async_remote_copy(
            src_ref=src, dst_ref=dst, send_sem=send.at[slot], recv_sem=recv.at[slot],
            device_id={"dp": device}, device_id_type=pl.DeviceIdType.MESH)

    sent, taken, kept = [], [0], [0]

    def slots(count):
        taken[0] += count
        return list(range(taken[0] - count, taken[0]))

    def go(src, dst, slot, device):
        c = copy(src, dst, slot, device)
        c.start()
        sent.append(c)

    def keep(src, dst):
        c = pltpu.make_async_copy(src, dst, own.at[kept[0]])
        kept[0] += 1
        c.start()
        return c

    class Gather:
        def __init__(self, pay, near, rows, columns):
            self.pay, self.near, self.rows, self.columns = pay, near, rows, columns
            self.n, self.z, self.x = slots(7), slots(3), slots(6)

        def near_start(self):
            self.mine = keep(self.pay.at[quarter], self.near.at[line])
            for r in range(1, 8):
                go(self.pay.at[(line + r) % 4], self.near.at[line], self.n[r - 1], near_dev(r))

        def near_wait(self):
            self.mine.wait()
            for r in range(1, 8):
                copy(self.pay.at[0], self.near.at[(line + 8 - r) % 8], self.n[r - 1], near_dev(r)).wait_recv()
            for at in range(0, self.columns, 512):
                size = min(512, self.columns - at)
                index = lax.broadcasted_iota(jnp.int32, (16, size), 0)
                block = jnp.zeros((16, size), f32)
                for s in range(8):
                    pair = self.near[s, :, at:at + size].astype(f32)
                    for k in range(2):
                        block = jnp.where(index == 2 * s + k, pair[k:k + 1], block)
                self.rows[zpos, xpos, :, at:at + size] = block.astype(bf16)

        def z_start(self):
            for r in range(1, 4):
                go(self.rows.at[zpos, xpos], self.rows.at[zpos, xpos], self.z[r - 1], z_dev(r))

        def z_wait(self):
            for r in range(1, 4):
                copy(self.rows.at[zpos, xpos], self.rows.at[(zpos + 4 - r) % 4, xpos], self.z[r - 1], z_dev(r)).wait_recv()

        def piece(self, top, x):
            return self.rows.at[pl.ds(2 * top, 2), x]

        def x_start(self):
            go(self.piece(0, xpos), self.piece(0, xpos), self.x[0], x_dev(1))
            go(self.piece(1, xpos), self.piece(1, xpos), self.x[1], x_dev(3))
            go(self.piece(1, xpos), self.piece(1, xpos), self.x[2], x_dev(1))
            go(self.piece(0, xpos), self.piece(0, xpos), self.x[3], x_dev(3))

        def x_pass(self):
            copy(self.piece(0, xpos), self.piece(0, behind), self.x[0], x_dev(1)).wait_recv()
            go(self.piece(0, behind), self.piece(0, behind), self.x[4], x_dev(1))
            copy(self.piece(1, xpos), self.piece(1, ahead), self.x[1], x_dev(3)).wait_recv()
            go(self.piece(1, ahead), self.piece(1, ahead), self.x[5], x_dev(3))

        def x_wait(self):
            copy(self.piece(1, xpos), self.piece(1, behind), self.x[2], x_dev(1)).wait_recv()
            copy(self.piece(0, xpos), self.piece(0, ahead), self.x[3], x_dev(3)).wait_recv()
            copy(self.piece(0, xpos), self.piece(0, across), self.x[4], x_dev(1)).wait_recv()
            copy(self.piece(1, xpos), self.piece(1, across), self.x[5], x_dev(3)).wait_recv()

    ys = ref["yr"]
    gy = Gather(pay_y, ref["ny"], ys, part)
    if first_step:
        xs = ref["xr"]
        gx = Gather(ref["pay_x"], ref["nx"], xs, wide)
        later = Gather(ref["pay_l"], ref["nl"], ref["lr"], wide)
        now = (gx, gy)
    else:
        xs = ref["xr_in"]
        now = (gy,)
    for g in now:
        g.near_start()
    if first_step:
        later.near_start()
    for g in now:
        g.near_wait()
        g.z_start()
    if first_step:
        later.near_wait()
    for g in now:
        g.z_wait()
        g.x_start()
    if first_step:
        later.z_start()
    for g in now:
        g.x_pass()
    for g in now:
        g.x_wait()
    if first_step:
        later.z_wait()
        later.x_start()

    xmat = xs[:, :, :, 0:part].reshape(256, part)
    pu, ra, sb, rb, dd = ref["pu"], ref["ra"], ref["sb"], ref["rb"], ref["dd"]
    pre = jnp.dot(xmat, w_in[...], preferred_element_type=f32)
    pu[:, :, 0:hidden] = pre.reshape(4, 64, hidden)
    upper = lax.dot_general(ys[...].reshape(256, part), w_out[...], (((1,), (1,)), ((), ())), preferred_element_type=f32)
    pu[:, :, hidden:2 * hidden] = upper.reshape(4, 64, hidden)

    s1, s2, s3, s4 = slots(4)
    go(pu.at[pl.ds(2 * (1 - core), 2)], ra, s1, core_dev)
    copy(pu.at[pl.ds(2 * (1 - core), 2)], ra, s1, core_dev).wait_recv()
    sb[...] = pu[pl.ds(2 * core, 2)] + ra[...]
    go(sb.at[1 - odd], rb, s2, odd_dev)
    if first_step:
        later.x_pass()
    copy(sb.at[1 - odd], rb, s2, odd_dev).wait_recv()
    k = 2 * core + odd
    both = sb[odd] + rb[...]
    pre = both[:, 0:hidden]
    upper = both[:, hidden:2 * hidden]
    gate = xs[k, :, :, part:wide].reshape(64, EXT).astype(f32)[:, 0:1]
    sig = jax.nn.sigmoid(pre)
    act = pre * sig
    dd[k, :, 0:hidden] = (gate * upper * (sig * (1.0 + pre * (1.0 - sig)))).astype(bf16)
    dd[k, :, hidden:2 * hidden] = (gate * act).astype(bf16)
    sums = jnp.sum(act * upper, axis=1, keepdims=True)
    dd[k, :, 2 * hidden:2 * hidden + EXT] = jnp.broadcast_to(sums, (64, EXT)).astype(bf16)
    go(dd.at[k], dd.at[k], s3, odd_dev)
    copy(dd.at[k], dd.at[2 * core + 1 - odd], s3, odd_dev).wait_recv()
    go(dd.at[pl.ds(2 * core, 2)], dd.at[pl.ds(2 * core, 2)], s4, core_dev)
    copy(dd.at[pl.ds(2 * core, 2)], dd.at[pl.ds(2 * (1 - core), 2)], s4, core_dev).wait_recv()

    ax, az, ah = ref["ax"], ref["az"], ref["ah"]
    sums = dd[:, :, 2 * hidden:2 * hidden + EXT].reshape(256, EXT)
    pick = (lax.broadcasted_iota(jnp.int32, (16, EXT), 1) == 0).astype(f32).astype(bf16)
    ax[xpos] = lax.dot_general(pick, sums, (((1,), (1,)), ((), ())), preferred_element_type=f32)[0:8]
    sx, sz = slots(3), slots(3)
    sh, = slots(1)
    for r in range(1, 4):
        go(ax.at[xpos], ax.at[xpos], sx[r - 1], x_dev(r))

    dx, rx, ry, dz, rz = ref["dx"], ref["rx"], ref["ry"], ref["dz"], ref["rz"]
    dpre = dd[:, :, 0:hidden].reshape(256, hidden)
    scaled = dd[:, :, hidden:2 * hidden].reshape(256, hidden)
    term = lax.dot_general(dpre, w_in[...], (((1,), (1,)), ((), ())), preferred_element_type=f32)
    dx[:, :, :, 0:part] = term.astype(bf16).reshape(4, 4, 16, part)
    lanes = lax.broadcasted_iota(jnp.int32, (256, EXT), 1)
    sums = jnp.where(lanes < EXT // 2, sums.astype(f32), 0.0)
    dx[:, :, :, part:wide] = sums.astype(bf16).reshape(4, 4, 16, EXT)

    def piece(top, x):
        return dx.at[pl.ds(2 * top, 2), x]

    if first_step:
        later.x_wait()
    b = slots(6)
    go(piece(0, across), ry.at[0], b[0], x_dev(1))
    go(piece(1, across), ry.at[1], b[1], x_dev(3))
    go(piece(1, ahead), rx.at[0, pl.ds(2, 2)], b[2], x_dev(1))
    go(piece(0, behind), rx.at[1, pl.ds(0, 2)], b[3], x_dev(3))
    for r in range(1, 4):
        copy(ax.at[xpos], ax.at[(xpos + 4 - r) % 4], sx[r - 1], x_dev(r)).wait_recv()
    az[zpos] = ax[0] + ax[1] + ax[2] + ax[3]
    for r in range(1, 4):
        go(az.at[zpos], az.at[zpos], sz[r - 1], z_dev(r))

    def joined(first, second):
        value = first.astype(f32) + second.astype(f32)
        column = value[..., part:part + 1] + value[..., part + EXT // 2:part + EXT // 2 + 1]
        return value[..., 0:part].astype(bf16), split_ext(column).astype(bf16)

    def pass_on(top, x, slot, came, device):
        copy(piece(top, x), ry.at[came], slot, device).wait_recv()
        for z in range(2):
            main, ext = joined(dx[2 * top + z, x], ry[came, z])
            dx[2 * top + z, x, :, 0:part] = main
            dx[2 * top + z, x, :, part:wide] = ext

    pass_on(0, ahead, b[0], 0, x_dev(1))
    go(piece(0, ahead), rx.at[0, pl.ds(0, 2)], b[4], x_dev(1))
    pass_on(1, behind, b[1], 1, x_dev(3))
    go(piece(1, behind), rx.at[1, pl.ds(2, 2)], b[5], x_dev(3))
    one = lax.dot_general(xmat, dpre, (((0,), (0,)), ((), ())), preferred_element_type=f32)
    two = lax.dot_general(scaled, ys[...].reshape(256, part), (((0,), (0,)), ((), ())), preferred_element_type=f32)
    gin, gout = ref["gin"], ref["gout"]
    if first_step:
        gin[...] = one
        gout[...] = two
        ref["xr_out"][...] = ref["lr"][...]
    else:
        gin[...] = (ref["acc_in"][...] + one).astype(bf16)
        gout[...] = (ref["acc_out"][...] + two).astype(bf16)
    for r in range(1, 4):
        copy(az.at[zpos], az.at[(zpos + 4 - r) % 4], sz[r - 1], z_dev(r)).wait_recv()
    ah[half] = az[0] + az[1] + az[2] + az[3]
    go(ah.at[half], ah.at[half], sh, half_dev)
    copy(piece(1, xpos), rx.at[0, pl.ds(2, 2)], b[2], x_dev(1)).wait_recv()
    copy(piece(0, xpos), rx.at[1, pl.ds(0, 2)], b[3], x_dev(3)).wait_recv()
    copy(piece(0, xpos), rx.at[0, pl.ds(0, 2)], b[4], x_dev(1)).wait_recv()
    copy(piece(1, xpos), rx.at[1, pl.ds(2, 2)], b[5], x_dev(3)).wait_recv()
    for z in range(4):
        value = dx[z, xpos].astype(f32) + rx[0, z].astype(f32) + rx[1, z].astype(f32)
        dz[z, :, 0:part] = value[:, 0:part].astype(bf16)
        column = value[:, part:part + 1] + value[:, part + EXT // 2:part + EXT // 2 + 1]
        dz[z, :, part:wide] = split_ext(column).astype(bf16)
    e = slots(3)
    for r in range(1, 4):
        go(dz.at[(zpos + r) % 4], rz.at[r - 1], e[r - 1], z_dev(r))
    copy(ah.at[half], ah.at[1 - half], sh, half_dev).wait_recv()
    dgate = (ah[0] + ah[1])[0:1]
    ext = jnp.transpose(xs[:, :, :, part:wide].reshape(256, EXT).astype(f32))
    slope = ext[8:16] + ext[16:24] + ext[24:32]
    dlog = slope * dgate
    high = rounded(dlog)
    middle = rounded(dlog - high)
    split = jnp.concatenate([high, middle, dlog - high - middle, jnp.zeros_like(high)], axis=0).astype(bf16)
    router = jnp.dot(split, xmat, preferred_element_type=f32)
    router = router[0:8] + router[8:16] + router[16:24]
    if first_step:
        ref["gr"][...] = router
    else:
        mine, parts = ref["mine"], ref["parts"]
        mine[...] = ref["gr_in"][...] + router
        held = keep(mine, parts.at[quarter])
        qs = slots(3)
        for r in range(1, 4):
            go(mine, parts.at[quarter], qs[r - 1], base + half * 4 + (quarter + r) % 4)
    for r in range(1, 4):
        copy(dz.at[0], rz.at[r - 1], e[r - 1], z_dev(r)).wait_recv()
    fin, split, rf = ref["fin"], ref["split"], ref["rf"]
    value = dz[zpos].astype(f32)
    for r in range(3):
        value = value + rz[r].astype(f32)
    fin[:, 0:part] = value[:, 0:part]
    column = value[:, part:part + 1] + value[:, part + EXT // 2:part + EXT // 2 + 1]
    fin[:, part:wide] = jnp.broadcast_to(column, (16, EXT))
    for s in range(8):
        split[s] = fin[2 * s:2 * s + 2, :]
    stay = keep(split.at[line], rf.at[line])
    n = slots(7)
    for r in range(1, 8):
        go(split.at[(line + r) % 8], rf.at[line], n[r - 1], near_dev(r))
    stay.wait()
    for r in range(1, 8):
        copy(split.at[0], rf.at[(line + 8 - r) % 8], n[r - 1], near_dev(r)).wait_recv()
    ref["back"][...] = rf[0:4] + rf[4:8]
    if not first_step:
        held.wait()
        for r in range(1, 4):
            copy(mine, parts.at[(quarter + 4 - r) % 4], qs[r - 1], core_dev).wait_recv()
        ref["gr"][...] = parts[...]
    for c in sent:
        c.wait_send()


def run_step(first_step, experts, ins):
    part, hidden = ins["w_in"].shape
    wide = part + EXT
    bf16, f32 = jnp.bfloat16, jnp.float32
    grad = f32 if first_step else bf16
    outs = {
        "back": ((4, CAP, wide), f32),
        "gin": ((part, hidden), grad),
        "gout": ((hidden, part), grad),
        "gr": ((experts, part) if first_step else (4, experts, part), f32),
    }
    scratch = {
        "ny": ((8, CAP, part), bf16),
        "yr": ((4, 4, 16, part), bf16),
        "pu": ((4, 64, 2 * hidden), f32),
        "ra": ((2, 64, 2 * hidden), f32),
        "sb": ((2, 64, 2 * hidden), f32),
        "rb": ((64, 2 * hidden), f32),
        "dd": ((4, 64, 2 * hidden + EXT), bf16),
        "dx": ((4, 4, 16, wide), bf16),
        "rx": ((2, 4, 16, wide), bf16),
        "ry": ((2, 2, 16, wide), bf16),
        "dz": ((4, 16, wide), bf16),
        "rz": ((3, 16, wide), bf16),
        "ax": ((4, 8, 256), f32),
        "az": ((4, 8, 256), f32),
        "ah": ((2, 8, 256), f32),
        "fin": ((16, wide), f32),
        "split": ((8, CAP, wide), f32),
        "rf": ((8, CAP, wide), f32),
    }
    if first_step:
        outs["xr_out"] = ((4, 4, 16, wide), bf16)
        scratch["nx"] = scratch["nl"] = ((8, CAP, wide), bf16)
        scratch["xr"] = scratch["lr"] = ((4, 4, 16, wide), bf16)
    else:
        scratch["mine"] = ((experts, part), f32)
        scratch["parts"] = ((4, experts, part), f32)
    names = list(ins) + list(outs) + list(scratch) + ["send", "recv", "own"]
    vmem = pl.BlockSpec(memory_space=pltpu.VMEM)
    copies = 80
    got = pl.pallas_call(
        functools.partial(step_kernel, first_step, part, hidden, experts, names),
        out_shape=[jax.ShapeDtypeStruct(*leaf) for leaf in outs.values()],
        in_specs=[vmem] * len(ins),
        out_specs=[vmem] * len(outs),
        scratch_shapes=[pltpu.VMEM(*leaf) for leaf in scratch.values()]
        + [pltpu.SemaphoreType.DMA((copies,)), pltpu.SemaphoreType.DMA((copies,)), pltpu.SemaphoreType.DMA((8,))],
        compiler_params=pltpu.CompilerParams(
            collective_id=0 if first_step else 1, has_side_effects=True, vmem_limit_bytes=48 << 20
        ),
    )(*ins.values())
    return dict(zip(outs, got))


def local(saved_inputs, carried, head_grad, routing, replica_counts, router, w_in, w_out):
    hi = lax.Precision.HIGHEST
    section_count = lax.axis_size("section")
    section_index = lax.axis_index("section")
    dev_index = lax.axis_index("dp")
    width = head_grad.shape[1]
    part = w_in.shape[2]
    experts = router.shape[2]
    router_w = router[0]
    my_count = replica_counts[dev_index]
    first = (jnp.arange(experts) == 0).astype(jnp.float32)
    slots = jnp.arange(CAP, dtype=jnp.int32)

    def quarters(rows):
        return rows.reshape(CAP, 4, part).transpose(1, 0, 2)

    def prepare(step):
        xin = saved_inputs[0, step]
        ids = routing[0, step]
        live = step + section_index < my_count
        xf = xin.astype(jnp.float32)
        logits = jnp.dot(xf, router_w, precision=hi)
        expo = jnp.exp(logits)
        prob = expo / jnp.sum(expo, axis=1, keepdims=True)
        routed = ((ids[:, 0] == 0) | (ids[:, 1] == 0)) & live
        slot = jnp.cumsum(routed.astype(jnp.int32), dtype=jnp.int32) - 1
        table = ((slot[None, :] == slots[:, None]) & routed[None, :]).astype(jnp.float32)
        xs = jnp.dot(table.astype(jnp.bfloat16), xin, preferred_element_type=jnp.float32).astype(jnp.bfloat16)
        gate = jnp.dot(table, prob[:, 0], precision=hi).astype(jnp.bfloat16)
        slope = jnp.dot(table, prob[:, :1] * (first[None, :] - prob), precision=hi)
        high = rounded(slope)
        middle = rounded(slope - high)
        low = rounded(slope - high - middle)
        ext = jnp.concatenate(
            [jnp.broadcast_to(gate.astype(jnp.float32)[:, None], (CAP, 8)), high, middle, low], axis=1)
        ext = jnp.pad(ext, ((0, 0), (0, EXT - ext.shape[1]))).astype(jnp.bfloat16)
        payload = jnp.concatenate([quarters(xs), jnp.broadcast_to(ext[None], (4, CAP, EXT))], axis=2)
        return (prob, table, live, payload)

    prepared = [prepare(step) for step in range(STEPS)]
    outputs = []
    incoming = carried[0]
    weights = {"w_in": w_in[0, 0], "w_out": w_out[0, 0]}
    for step in range(STEPS):
        prob, table, live, payload = prepared[step]
        if step == 1:
            passed = shifted(outputs[0], "section", -1)
            incoming = jnp.where(section_index == section_count - 1, head_grad, passed)
        grad_in_tok = jnp.where(live, incoming, jnp.zeros_like(incoming))
        ys = jnp.dot(table.astype(jnp.bfloat16), grad_in_tok, preferred_element_type=jnp.float32).astype(jnp.bfloat16)
        ins = {"pay_y": quarters(ys), **weights}
        if step == 0:
            ins.update(pay_x=payload, pay_l=prepared[1][3])
        else:
            ins.update(xr_in=got["xr_out"], acc_in=got["gin"], acc_out=got["gout"], gr_in=got["gr"])
        got = run_step(step == 0, experts, ins)
        back = got["back"]
        dxs = back[:, :, :part].transpose(1, 0, 2).reshape(CAP, width)
        dgate = back[0, :, part]
        dxe = lax.dot_general(table, dxs, (((0,), (0,)), ((), ())), precision=hi)
        dg_tok = lax.dot_general(table, dgate, (((0,), (0,)), ((), ())), precision=hi)
        dlog = (dg_tok * prob[:, 0])[:, None] * (first[None, :] - prob)
        result = grad_in_tok.astype(jnp.float32) + dxe + jnp.dot(dlog, router_w.T, precision=hi)
        outputs.append(result.astype(jnp.bfloat16))
    grad_router = got["gr"].transpose(0, 2, 1).reshape(width, experts)
    return (jnp.stack(outputs)[:, None], got["gin"][None, None], got["gout"][None, None], grad_router[None])


def solution(mesh):
    in_specs = (
        P("section", None, "dp", None),
        P("section", "dp", None),
        P("dp", None),
        P("section", None, "dp", None),
        P(),
        P("section", None, None),
        P("section", "dp", None, None),
        P("section", "dp", None, None),
    )
    out_specs = (
        P(None, "section", "dp", None),
        P("section", "dp", None, None),
        P("section", "dp", None, None),
        P("section", None, None),
    )
    return jax.shard_map(local, mesh=mesh, in_specs=in_specs, out_specs=out_specs, check_vma=False)
```

```python
import functools

import jax
import jax.numpy as jnp
from jax import lax
from jax.experimental import pallas as pl
from jax.experimental.pallas import tpu as pltpu
from jax.sharding import PartitionSpec as P

STEPS = 2
CAP = 2
EXT = 128


def rounded(value):
    return value.astype(jnp.bfloat16).astype(jnp.float32)


def split_ext(value):
    lanes = lax.broadcasted_iota(jnp.int32, value.shape[:-1] + (EXT,), len(value.shape) - 1)
    high = rounded(value)
    return jnp.where(lanes < EXT // 2, high, value - high)


def window_kernel(part, hidden, experts, sections, names, *refs):
    ref = dict(zip(names, refs))
    w_in, w_out = ref["w_in"], ref["w_out"]
    send, recv, own = ref["send"], ref["recv"], ref["own"]
    wide = part + EXT
    f32, bf16 = jnp.float32, jnp.bfloat16
    me = lax.axis_index("dp")
    section = lax.axis_index("section")
    before, after = (section + sections - 1) % sections, (section + 1) % sections
    line = me % 8
    base = me - line
    core = me % 2
    odd = (me // 2) % 2
    half = line // 4
    quarter = me % 4
    xpos = (me // 8) % 4
    zpos = me // 32
    ahead, behind, across = (xpos + 1) % 4, (xpos + 3) % 4, (xpos + 2) % 4

    def near_dev(r):
        return base + (line + r) % 8

    def z_dev(r):
        return ((zpos + r) % 4) * 32 + xpos * 8 + line

    def x_dev(r):
        return zpos * 32 + ((xpos + r) % 4) * 8 + line

    core_dev = base + (line // 2) * 2 + (1 - core)
    odd_dev = base + half * 4 + (1 - odd) * 2 + core
    half_dev = base + (line + 4) % 8

    barrier = pltpu.get_barrier_semaphore()
    peers = [near_dev(r) for r in range(1, 8)]
    peers += [z_dev(r) for r in range(1, 4)] + [x_dev(r) for r in range(1, 4)]
    for peer in peers:
        pl.semaphore_signal(barrier, inc=1, device_id={"dp": peer}, device_id_type=pl.DeviceIdType.MESH)
    for neighbour in (before, after):
        pl.semaphore_signal(
            barrier, inc=1, device_id={"section": neighbour}, device_id_type=pl.DeviceIdType.MESH)
    pl.semaphore_wait(barrier, len(peers) + 2)

    def copy(src, dst, slot, device):
        return pltpu.make_async_remote_copy(
            src_ref=src, dst_ref=dst, send_sem=send.at[slot], recv_sem=recv.at[slot],
            device_id={"dp": device}, device_id_type=pl.DeviceIdType.MESH)

    def copy_section(src, dst, slot, target):
        return pltpu.make_async_remote_copy(
            src_ref=src, dst_ref=dst, send_sem=send.at[slot], recv_sem=recv.at[slot],
            device_id={"section": target}, device_id_type=pl.DeviceIdType.MESH)

    sent, taken, kept = [], [0], [0]

    def slots(count):
        taken[0] += count
        return list(range(taken[0] - count, taken[0]))

    def go(src, dst, slot, device):
        c = copy(src, dst, slot, device)
        c.start()
        sent.append(c)

    def keep(src, dst):
        c = pltpu.make_async_copy(src, dst, own.at[kept[0]])
        kept[0] += 1
        c.start()
        return c

    class Gather:
        def __init__(self, pay, near, rows, columns):
            self.pay, self.near, self.rows, self.columns = pay, near, rows, columns
            self.n, self.z, self.x = slots(7), slots(3), slots(6)

        def near_start(self):
            self.mine = keep(self.pay.at[quarter], self.near.at[line])
            for r in range(1, 8):
                go(self.pay.at[(line + r) % 4], self.near.at[line], self.n[r - 1], near_dev(r))

        def near_wait(self):
            self.mine.wait()
            for r in range(1, 8):
                copy(self.pay.at[0], self.near.at[(line + 8 - r) % 8], self.n[r - 1], near_dev(r)).wait_recv()
            for at in range(0, self.columns, 512):
                size = min(512, self.columns - at)
                index = lax.broadcasted_iota(jnp.int32, (16, size), 0)
                block = jnp.zeros((16, size), f32)
                for s in range(8):
                    pair = self.near[s, :, at:at + size].astype(f32)
                    for k in range(2):
                        block = jnp.where(index == 2 * s + k, pair[k:k + 1], block)
                self.rows[zpos, xpos, :, at:at + size] = block.astype(bf16)

        def z_start(self):
            for r in range(1, 4):
                go(self.rows.at[zpos, xpos], self.rows.at[zpos, xpos], self.z[r - 1], z_dev(r))

        def z_wait(self):
            for r in range(1, 4):
                copy(self.rows.at[zpos, xpos], self.rows.at[(zpos + 4 - r) % 4, xpos], self.z[r - 1], z_dev(r)).wait_recv()

        def piece(self, top, x):
            return self.rows.at[pl.ds(2 * top, 2), x]

        def x_start(self):
            go(self.piece(0, xpos), self.piece(0, xpos), self.x[0], x_dev(1))
            go(self.piece(1, xpos), self.piece(1, xpos), self.x[1], x_dev(3))
            go(self.piece(1, xpos), self.piece(1, xpos), self.x[2], x_dev(1))
            go(self.piece(0, xpos), self.piece(0, xpos), self.x[3], x_dev(3))

        def x_pass(self):
            copy(self.piece(0, xpos), self.piece(0, behind), self.x[0], x_dev(1)).wait_recv()
            go(self.piece(0, behind), self.piece(0, behind), self.x[4], x_dev(1))
            copy(self.piece(1, xpos), self.piece(1, ahead), self.x[1], x_dev(3)).wait_recv()
            go(self.piece(1, ahead), self.piece(1, ahead), self.x[5], x_dev(3))

        def x_wait(self):
            copy(self.piece(1, xpos), self.piece(1, behind), self.x[2], x_dev(1)).wait_recv()
            copy(self.piece(0, xpos), self.piece(0, ahead), self.x[3], x_dev(3)).wait_recv()
            copy(self.piece(0, xpos), self.piece(0, across), self.x[4], x_dev(1)).wait_recv()
            copy(self.piece(1, xpos), self.piece(1, across), self.x[5], x_dev(3)).wait_recv()

    tabs, slopes, router_t, head = ref["tabs"], ref["slopes"], ref["router_t"], ref["head"]
    is_last = section == sections - 1
    s_tab, s_rows, s_full = slots(3)
    c = copy_section(tabs.at[1], ref["tab_next"], s_tab, after)
    c.start()
    sent.append(c)
    gx = Gather(ref["pay_x"], ref["nx"], ref["xr"], wide)
    later = Gather(ref["pay_l"], ref["nl"], ref["lr"], wide)

    def slot_rows(table, rows):
        picked = [jnp.sum(table[:, c:c + 1] * rows, axis=0, keepdims=True) for c in range(CAP)]
        index = lax.broadcasted_iota(jnp.int32, (CAP, part), 0)
        return jnp.where(index == 0, picked[0], picked[1]).astype(bf16)

    def finish(step, dy, out):
        rf = ref[f"rf{step}"]
        dgate = rf[0, :, part:wide] + rf[4, :, part:wide]
        for q in range(4):
            rows = rf[q, :, 0:part] + rf[q + 4, :, 0:part]
            result = dy(q)
            for c in range(CAP):
                dlog = slopes[step, :, c:c + 1] * dgate[c:c + 1, 0:1]
                row = rows[c:c + 1] + jnp.sum(dlog * router_t[q], axis=0, keepdims=True)
                result = result + tabs[step, :, c:c + 1] * row
            out[q] = result.astype(bf16)

    def one_step(step):
        first_step = step == 0
        local_ref = lambda name: ref[f"{name}{step}"]
        ys = local_ref("yr")
        gy = Gather(ref["pay_y"] if first_step else ref["pay1"], local_ref("ny"), ys, part)
        xs = ref["xr"] if first_step else ref["lr"]
        now = (gx, gy) if first_step else (gy,)
        for g in now:
            g.near_start()
        if first_step:
            later.near_start()
        for g in now:
            g.near_wait()
            g.z_start()
        if first_step:
            later.near_wait()
        for g in now:
            g.z_wait()
            g.x_start()
        if first_step:
            later.z_start()
        else:
            c = copy_section(ref["res0"], ref["inc"], s_full, before)
            c.start()
            sent.append(c)
        for g in now:
            g.x_pass()
        for g in now:
            g.x_wait()
        if first_step:
            later.z_wait()
            later.x_start()

        xmat = xs[:, :, :, 0:part].reshape(256, part)
        pu, ra, sb, rb, dd = local_ref("pu"), local_ref("ra"), local_ref("sb"), local_ref("rb"), local_ref("dd")
        pre = jnp.dot(xmat, w_in[...], preferred_element_type=f32)
        pu[:, :, 0:hidden] = pre.reshape(4, 64, hidden)
        upper = lax.dot_general(ys[...].reshape(256, part), w_out[...], (((1,), (1,)), ((), ())), preferred_element_type=f32)
        pu[:, :, hidden:2 * hidden] = upper.reshape(4, 64, hidden)

        s1, s2, s3, s4 = slots(4)
        go(pu.at[pl.ds(2 * (1 - core), 2)], ra, s1, core_dev)
        copy(pu.at[pl.ds(2 * (1 - core), 2)], ra, s1, core_dev).wait_recv()
        sb[...] = pu[pl.ds(2 * core, 2)] + ra[...]
        go(sb.at[1 - odd], rb, s2, odd_dev)
        if first_step:
            later.x_pass()
        copy(sb.at[1 - odd], rb, s2, odd_dev).wait_recv()
        k = 2 * core + odd
        both = sb[odd] + rb[...]
        pre = both[:, 0:hidden]
        upper = both[:, hidden:2 * hidden]
        gate = xs[k, :, :, part:wide].reshape(64, EXT).astype(f32)[:, 0:1]
        sig = jax.nn.sigmoid(pre)
        act = pre * sig
        dd[k, :, 0:hidden] = (gate * upper * (sig * (1.0 + pre * (1.0 - sig)))).astype(bf16)
        dd[k, :, hidden:2 * hidden] = (gate * act).astype(bf16)
        sums = jnp.sum(act * upper, axis=1, keepdims=True)
        dd[k, :, 2 * hidden:2 * hidden + EXT] = jnp.broadcast_to(sums, (64, EXT)).astype(bf16)
        go(dd.at[k], dd.at[k], s3, odd_dev)
        copy(dd.at[k], dd.at[2 * core + 1 - odd], s3, odd_dev).wait_recv()
        go(dd.at[pl.ds(2 * core, 2)], dd.at[pl.ds(2 * core, 2)], s4, core_dev)
        copy(dd.at[pl.ds(2 * core, 2)], dd.at[pl.ds(2 * (1 - core), 2)], s4, core_dev).wait_recv()

        ax, az, ah = local_ref("ax"), local_ref("az"), local_ref("ah")
        sums = dd[:, :, 2 * hidden:2 * hidden + EXT].reshape(256, EXT)
        pick = (lax.broadcasted_iota(jnp.int32, (16, EXT), 1) == 0).astype(f32).astype(bf16)
        ax[xpos] = lax.dot_general(pick, sums, (((1,), (1,)), ((), ())), preferred_element_type=f32)[0:8]
        sx, sz = slots(3), slots(3)
        sh, = slots(1)
        for r in range(1, 4):
            go(ax.at[xpos], ax.at[xpos], sx[r - 1], x_dev(r))

        dx, rx, ry, dz, rz = local_ref("dx"), local_ref("rx"), local_ref("ry"), local_ref("dz"), local_ref("rz")
        dpre = dd[:, :, 0:hidden].reshape(256, hidden)
        scaled = dd[:, :, hidden:2 * hidden].reshape(256, hidden)
        term = lax.dot_general(dpre, w_in[...], (((1,), (1,)), ((), ())), preferred_element_type=f32)
        dx[:, :, :, 0:part] = term.astype(bf16).reshape(4, 4, 16, part)
        lanes = lax.broadcasted_iota(jnp.int32, (256, EXT), 1)
        sums = jnp.where(lanes < EXT // 2, sums.astype(f32), 0.0)
        dx[:, :, :, part:wide] = sums.astype(bf16).reshape(4, 4, 16, EXT)

        def piece(top, x):
            return dx.at[pl.ds(2 * top, 2), x]

        if first_step:
            later.x_wait()
        b = slots(6)
        go(piece(0, across), ry.at[0], b[0], x_dev(1))
        go(piece(1, across), ry.at[1], b[1], x_dev(3))
        go(piece(1, ahead), rx.at[0, pl.ds(2, 2)], b[2], x_dev(1))
        go(piece(0, behind), rx.at[1, pl.ds(0, 2)], b[3], x_dev(3))
        for r in range(1, 4):
            copy(ax.at[xpos], ax.at[(xpos + 4 - r) % 4], sx[r - 1], x_dev(r)).wait_recv()
        az[zpos] = ax[0] + ax[1] + ax[2] + ax[3]
        for r in range(1, 4):
            go(az.at[zpos], az.at[zpos], sz[r - 1], z_dev(r))

        def joined(first, second):
            value = first.astype(f32) + second.astype(f32)
            column = value[..., part:part + 1] + value[..., part + EXT // 2:part + EXT // 2 + 1]
            return value[..., 0:part].astype(bf16), split_ext(column).astype(bf16)

        def pass_on(top, x, slot, came, device):
            copy(piece(top, x), ry.at[came], slot, device).wait_recv()
            for z in range(2):
                main, ext = joined(dx[2 * top + z, x], ry[came, z])
                dx[2 * top + z, x, :, 0:part] = main
                dx[2 * top + z, x, :, part:wide] = ext

        pass_on(0, ahead, b[0], 0, x_dev(1))
        go(piece(0, ahead), rx.at[0, pl.ds(0, 2)], b[4], x_dev(1))
        pass_on(1, behind, b[1], 1, x_dev(3))
        go(piece(1, behind), rx.at[1, pl.ds(2, 2)], b[5], x_dev(3))
        one = lax.dot_general(xmat, dpre, (((0,), (0,)), ((), ())), preferred_element_type=f32)
        two = lax.dot_general(scaled, ys[...].reshape(256, part), (((0,), (0,)), ((), ())), preferred_element_type=f32)
        if first_step:
            ref["acc_in"][...] = one
            ref["acc_out"][...] = two
        else:
            ref["gin"][...] = (ref["acc_in"][...] + one).astype(bf16)
            ref["gout"][...] = (ref["acc_out"][...] + two).astype(bf16)
        for r in range(1, 4):
            copy(az.at[zpos], az.at[(zpos + 4 - r) % 4], sz[r - 1], z_dev(r)).wait_recv()
        ah[half] = az[0] + az[1] + az[2] + az[3]
        go(ah.at[half], ah.at[half], sh, half_dev)
        copy(piece(1, xpos), rx.at[0, pl.ds(2, 2)], b[2], x_dev(1)).wait_recv()
        copy(piece(0, xpos), rx.at[1, pl.ds(0, 2)], b[3], x_dev(3)).wait_recv()
        copy(piece(0, xpos), rx.at[0, pl.ds(0, 2)], b[4], x_dev(1)).wait_recv()
        copy(piece(1, xpos), rx.at[1, pl.ds(2, 2)], b[5], x_dev(3)).wait_recv()
        for z in range(4):
            value = dx[z, xpos].astype(f32) + rx[0, z].astype(f32) + rx[1, z].astype(f32)
            dz[z, :, 0:part] = value[:, 0:part].astype(bf16)
            column = value[:, part:part + 1] + value[:, part + EXT // 2:part + EXT // 2 + 1]
            dz[z, :, part:wide] = split_ext(column).astype(bf16)
        e = slots(3)
        for r in range(1, 4):
            go(dz.at[(zpos + r) % 4], rz.at[r - 1], e[r - 1], z_dev(r))
        copy(ah.at[half], ah.at[1 - half], sh, half_dev).wait_recv()
        dgate = (ah[0] + ah[1])[0:1]
        ext = jnp.transpose(xs[:, :, :, part:wide].reshape(256, EXT).astype(f32))
        slope = ext[8:16] + ext[16:24] + ext[24:32]
        dlog = slope * dgate
        high = rounded(dlog)
        middle = rounded(dlog - high)
        split = jnp.concatenate([high, middle, dlog - high - middle, jnp.zeros_like(high)], axis=0).astype(bf16)
        router = jnp.dot(split, xmat, preferred_element_type=f32)
        router = router[0:8] + router[8:16] + router[16:24]
        if first_step:
            ref["acc_router"][...] = router
        else:
            mine, parts = ref["mine"], ref["parts"]
            mine[...] = ref["acc_router"][...] + router
            held = keep(mine, parts.at[quarter])
            qs = slots(3)
            for r in range(1, 4):
                go(mine, parts.at[quarter], qs[r - 1], base + half * 4 + (quarter + r) % 4)
        for r in range(1, 4):
            copy(dz.at[0], rz.at[r - 1], e[r - 1], z_dev(r)).wait_recv()
        fin, split, rf = local_ref("fin"), local_ref("split"), local_ref("rf")
        value = dz[zpos].astype(f32)
        for r in range(3):
            value = value + rz[r].astype(f32)
        fin[:, 0:part] = value[:, 0:part]
        column = value[:, part:part + 1] + value[:, part + EXT // 2:part + EXT // 2 + 1]
        fin[:, part:wide] = jnp.broadcast_to(column, (16, EXT))
        for s in range(8):
            split[s] = fin[2 * s:2 * s + 2, :]
        stay = keep(split.at[line], rf.at[line])
        n = slots(7)
        for r in range(1, 8):
            go(split.at[(line + r) % 8], rf.at[line], n[r - 1], near_dev(r))
        stay.wait()
        for r in range(1, 8):
            copy(split.at[0], rf.at[(line + 8 - r) % 8], n[r - 1], near_dev(r)).wait_recv()
        if not first_step:
            held.wait()
            for r in range(1, 4):
                copy(mine, parts.at[(quarter + 4 - r) % 4], qs[r - 1], core_dev).wait_recv()
            ref["gr"][...] = parts[...]

    one_step(0)
    res0 = ref["res0"]
    finish(0, lambda q: ref["dy0"][q], res0)
    copy_section(tabs.at[1], ref["tab_next"], s_tab, after).wait_recv()
    for q in range(4):
        ref["rows_out"][q] = slot_rows(ref["tab_next"][...], res0[q].astype(f32))
    c = copy_section(ref["rows_out"], ref["rows_in"], s_rows, before)
    c.start()
    sent.append(c)
    ref["out"][0] = res0[...]
    c.wait_recv()
    for q in range(4):
        own_rows = slot_rows(tabs[1], head[q]).astype(f32)
        ref["pay1"][q] = jnp.where(is_last, own_rows, ref["rows_in"][q].astype(f32)).astype(bf16)
    one_step(1)
    copy_section(res0, ref["inc"], s_full, before).wait_recv()
    live = tabs[1, :, CAP:CAP + 1] > 0.5
    finish(
        1,
        lambda q: jnp.where(live, jnp.where(is_last, head[q], ref["inc"][q].astype(f32)), 0.0),
        ref["out"].at[1],
    )
    for c in sent:
        c.wait_send()


def run_window(experts, sections, ins):
    part, hidden = ins["w_in"].shape
    wide = part + EXT
    bf16, f32 = jnp.bfloat16, jnp.float32
    tokens = ins["dy0"].shape[1]
    outs = {
        "out": ((STEPS, 4, tokens, part), bf16),
        "gin": ((part, hidden), bf16),
        "gout": ((hidden, part), bf16),
        "gr": ((4, experts, part), f32),
    }
    each = {
        "ny": ((8, CAP, part), bf16),
        "yr": ((4, 4, 16, part), bf16),
        "pu": ((4, 64, 2 * hidden), f32),
        "ra": ((2, 64, 2 * hidden), f32),
        "sb": ((2, 64, 2 * hidden), f32),
        "rb": ((64, 2 * hidden), f32),
        "dd": ((4, 64, 2 * hidden + EXT), bf16),
        "dx": ((4, 4, 16, wide), bf16),
        "rx": ((2, 4, 16, wide), bf16),
        "ry": ((2, 2, 16, wide), bf16),
        "dz": ((4, 16, wide), bf16),
        "rz": ((3, 16, wide), bf16),
        "ax": ((4, 8, 256), f32),
        "az": ((4, 8, 256), f32),
        "ah": ((2, 8, 256), f32),
        "fin": ((16, wide), f32),
        "split": ((8, CAP, wide), f32),
        "rf": ((8, CAP, wide), f32),
    }
    scratch = {f"{name}{step}": leaf for step in range(STEPS) for name, leaf in each.items()}
    scratch.update({
        "nx": ((8, CAP, wide), bf16),
        "nl": ((8, CAP, wide), bf16),
        "xr": ((4, 4, 16, wide), bf16),
        "lr": ((4, 4, 16, wide), bf16),
        "acc_in": ((part, hidden), f32),
        "acc_out": ((hidden, part), f32),
        "acc_router": ((experts, part), f32),
        "mine": ((experts, part), f32),
        "parts": ((4, experts, part), f32),
        "tab_next": ((tokens, 128), f32),
        "res0": ((4, tokens, part), bf16),
        "inc": ((4, tokens, part), bf16),
        "rows_out": ((4, CAP, part), bf16),
        "rows_in": ((4, CAP, part), bf16),
        "pay1": ((4, CAP, part), bf16),
    })
    names = list(ins) + list(outs) + list(scratch) + ["send", "recv", "own"]
    vmem = pl.BlockSpec(memory_space=pltpu.VMEM)
    copies = 160
    got = pl.pallas_call(
        functools.partial(window_kernel, part, hidden, experts, sections, names),
        out_shape=[jax.ShapeDtypeStruct(*leaf) for leaf in outs.values()],
        in_specs=[vmem] * len(ins),
        out_specs=[vmem] * len(outs),
        scratch_shapes=[pltpu.VMEM(*leaf) for leaf in scratch.values()]
        + [pltpu.SemaphoreType.DMA((copies,)), pltpu.SemaphoreType.DMA((copies,)), pltpu.SemaphoreType.DMA((8,))],
        compiler_params=pltpu.CompilerParams(
            collective_id=0, has_side_effects=True, vmem_limit_bytes=48 << 20
        ),
    )(*ins.values())
    return dict(zip(outs, got))


def local(saved_inputs, carried, head_grad, routing, replica_counts, router, w_in, w_out):
    hi = lax.Precision.HIGHEST
    section_index = lax.axis_index("section")
    dev_index = lax.axis_index("dp")
    width = head_grad.shape[1]
    part = w_in.shape[2]
    experts = router.shape[2]
    router_w = router[0]
    my_count = replica_counts[dev_index]
    first = (jnp.arange(experts) == 0).astype(jnp.float32)
    slots = jnp.arange(CAP, dtype=jnp.int32)

    def quarters(rows):
        return rows.reshape(CAP, 4, part).transpose(1, 0, 2)

    def prepare(step):
        xin = saved_inputs[0, step]
        ids = routing[0, step]
        live = step + section_index < my_count
        xf = xin.astype(jnp.float32)
        logits = jnp.dot(xf, router_w, precision=hi)
        expo = jnp.exp(logits)
        prob = expo / jnp.sum(expo, axis=1, keepdims=True)
        routed = ((ids[:, 0] == 0) | (ids[:, 1] == 0)) & live
        slot = jnp.cumsum(routed.astype(jnp.int32), dtype=jnp.int32) - 1
        table = ((slot[None, :] == slots[:, None]) & routed[None, :]).astype(jnp.float32)
        xs = jnp.dot(table.astype(jnp.bfloat16), xin, preferred_element_type=jnp.float32).astype(jnp.bfloat16)
        gate = jnp.dot(table, prob[:, 0], precision=hi).astype(jnp.bfloat16)
        slope = jnp.dot(table, prob[:, :1] * (first[None, :] - prob), precision=hi)
        high = rounded(slope)
        middle = rounded(slope - high)
        low = rounded(slope - high - middle)
        ext = jnp.concatenate(
            [jnp.broadcast_to(gate.astype(jnp.float32)[:, None], (CAP, 8)), high, middle, low], axis=1)
        ext = jnp.pad(ext, ((0, 0), (0, EXT - ext.shape[1]))).astype(jnp.bfloat16)
        payload = jnp.concatenate([quarters(xs), jnp.broadcast_to(ext[None], (4, CAP, EXT))], axis=2)
        column = jnp.concatenate([table.T, live.astype(jnp.float32) * jnp.ones((xin.shape[0], 1))], axis=1)
        column = jnp.pad(column, ((0, 0), (0, 128 - column.shape[1])))
        return (table, live, payload, column, jnp.pad(slope.T, ((0, 0), (0, 128 - CAP))))

    prepared = [prepare(step) for step in range(STEPS)]
    def token_quarters(rows):
        return rows.astype(jnp.float32).reshape(-1, 4, part).transpose(1, 0, 2)

    table, live, payload, *_ = prepared[0]
    dy = jnp.where(live, carried[0], jnp.zeros_like(carried[0]))
    ys = jnp.dot(table.astype(jnp.bfloat16), dy, preferred_element_type=jnp.float32).astype(jnp.bfloat16)
    got = run_window(experts, lax.axis_size("section"), {
        "w_in": w_in[0, 0],
        "w_out": w_out[0, 0],
        "pay_y": quarters(ys),
        "pay_x": payload,
        "pay_l": prepared[1][2],
        "dy0": token_quarters(dy),
        "head": token_quarters(head_grad),
        "tabs": jnp.stack([prepared[step][3] for step in range(STEPS)]),
        "slopes": jnp.stack([prepared[step][4] for step in range(STEPS)]),
        "router_t": router_w.T.reshape(experts, 4, part).transpose(1, 0, 2),
    })
    grad_router = got["gr"].transpose(0, 2, 1).reshape(width, experts)
    input_grad = got["out"].transpose(0, 2, 1, 3).reshape(STEPS, 1, -1, width)
    return (input_grad, got["gin"][None, None], got["gout"][None, None], grad_router[None])


def solution(mesh):
    in_specs = (
        P("section", None, "dp", None),
        P("section", "dp", None),
        P("dp", None),
        P("section", None, "dp", None),
        P(),
        P("section", None, None),
        P("section", "dp", None, None),
        P("section", "dp", None, None),
    )
    out_specs = (
        P(None, "section", "dp", None),
        P("section", "dp", None, None),
        P("section", "dp", None, None),
        P("section", None, None),
    )
    return jax.shard_map(local, mesh=mesh, in_specs=in_specs, out_specs=out_specs, check_vma=False)
```

```python
import functools

import jax
import jax.numpy as jnp
from jax import lax
from jax.experimental import pallas as pl
from jax.experimental.pallas import tpu as pltpu
from jax.sharding import PartitionSpec as P

STEPS = 2
CAP = 2
EXT = 128


def rounded(value):
    return value.astype(jnp.bfloat16).astype(jnp.float32)


def split_ext(value):
    lanes = lax.broadcasted_iota(jnp.int32, value.shape[:-1] + (EXT,), len(value.shape) - 1)
    high = rounded(value)
    return jnp.where(lanes < EXT // 2, high, value - high)


def window_kernel(part, hidden, experts, sections, names, *refs):
    ref = dict(zip(names, refs))
    w_in, w_out = ref["w_in"], ref["w_out"]
    send, recv, own = ref["send"], ref["recv"], ref["own"]
    wide = part + EXT
    f32, bf16 = jnp.float32, jnp.bfloat16
    me = lax.axis_index("dp")
    section = lax.axis_index("section")
    before, after = (section + sections - 1) % sections, (section + 1) % sections
    line = me % 8
    base = me - line
    core = me % 2
    odd = (me // 2) % 2
    half = line // 4
    quarter = me % 4
    xpos = (me // 8) % 4
    zpos = me // 32
    ahead, behind, across = (xpos + 1) % 4, (xpos + 3) % 4, (xpos + 2) % 4

    def near_dev(r):
        return base + (line + r) % 8

    def z_dev(r):
        return ((zpos + r) % 4) * 32 + xpos * 8 + line

    def x_dev(r):
        return zpos * 32 + ((xpos + r) % 4) * 8 + line

    core_dev = base + (line // 2) * 2 + (1 - core)
    odd_dev = base + half * 4 + (1 - odd) * 2 + core
    half_dev = base + (line + 4) % 8

    barrier = pltpu.get_barrier_semaphore()
    peers = [near_dev(r) for r in range(1, 8)]
    peers += [z_dev(r) for r in range(1, 4)] + [x_dev(r) for r in range(1, 4)]
    for peer in peers:
        pl.semaphore_signal(barrier, inc=1, device_id={"dp": peer}, device_id_type=pl.DeviceIdType.MESH)
    for neighbour in (before, after):
        pl.semaphore_signal(
            barrier, inc=1, device_id={"section": neighbour}, device_id_type=pl.DeviceIdType.MESH)
    pl.semaphore_wait(barrier, len(peers) + 2)

    def copy(src, dst, slot, device):
        return pltpu.make_async_remote_copy(
            src_ref=src, dst_ref=dst, send_sem=send.at[slot], recv_sem=recv.at[slot],
            device_id={"dp": device}, device_id_type=pl.DeviceIdType.MESH)

    def copy_section(src, dst, slot, target):
        return pltpu.make_async_remote_copy(
            src_ref=src, dst_ref=dst, send_sem=send.at[slot], recv_sem=recv.at[slot],
            device_id={"section": target}, device_id_type=pl.DeviceIdType.MESH)

    sent, taken, kept = [], [0], [0]

    def slots(count):
        taken[0] += count
        return list(range(taken[0] - count, taken[0]))

    def go(src, dst, slot, device):
        c = copy(src, dst, slot, device)
        c.start()
        sent.append(c)

    def keep(src, dst):
        c = pltpu.make_async_copy(src, dst, own.at[kept[0]])
        kept[0] += 1
        c.start()
        return c

    class Gather:
        def __init__(self, pay, near, rows, columns):
            self.pay, self.near, self.rows, self.columns = pay, near, rows, columns
            self.n, self.z, self.x = slots(7), slots(3), [slots(6), slots(6)]

        def near_start(self):
            self.mine = keep(self.pay.at[quarter], self.near.at[line])
            for r in range(1, 8):
                go(self.pay.at[(line + r) % 4], self.near.at[line], self.n[r - 1], near_dev(r))

        def near_wait(self):
            self.mine.wait()
            for r in range(1, 8):
                copy(self.pay.at[0], self.near.at[(line + 8 - r) % 8], self.n[r - 1], near_dev(r)).wait_recv()
            for at in range(0, self.columns, 512):
                size = min(512, self.columns - at)
                index = lax.broadcasted_iota(jnp.int32, (16, size), 0)
                block = jnp.zeros((16, size), f32)
                for s in range(8):
                    pair = self.near[s, :, at:at + size].astype(f32)
                    for k in range(2):
                        block = jnp.where(index == 2 * s + k, pair[k:k + 1], block)
                self.rows[zpos, xpos, :, at:at + size] = block.astype(bf16)

        def z_start(self):
            for r in range(1, 4):
                go(self.rows.at[zpos, xpos], self.rows.at[zpos, xpos], self.z[r - 1], z_dev(r))

        def z_wait(self):
            for r in range(1, 4):
                copy(self.rows.at[zpos, xpos], self.rows.at[(zpos + 4 - r) % 4, xpos], self.z[r - 1], z_dev(r)).wait_recv()

        def piece(self, t, top, x):
            return self.rows.at[2 * t + top, x]

        def came(self, t, top, x, slot, device):
            copy(self.piece(t, top, xpos), self.piece(t, top, x), self.x[t][slot], device).wait_recv()

        def give(self, t, top, x, slot, device):
            go(self.piece(t, top, x), self.piece(t, top, x), self.x[t][slot], device)

        def x_start(self, t):
            self.give(t, 0, xpos, 0, x_dev(1))
            self.give(t, 1, xpos, 1, x_dev(3))
            self.give(t, 1, xpos, 2, x_dev(1))
            self.give(t, 0, xpos, 3, x_dev(3))

        def x_pass(self, t):
            self.came(t, 0, behind, 0, x_dev(1))
            self.give(t, 0, behind, 4, x_dev(1))
            self.came(t, 1, ahead, 1, x_dev(3))
            self.give(t, 1, ahead, 5, x_dev(3))

        def x_wait(self, t):
            self.came(t, 1, behind, 2, x_dev(1))
            self.came(t, 0, ahead, 3, x_dev(3))
            self.came(t, 0, across, 4, x_dev(1))
            self.came(t, 1, across, 5, x_dev(3))

    tabs, slopes, router_t, head = ref["tabs"], ref["slopes"], ref["router_t"], ref["head"]
    is_last = section == sections - 1
    s_tab, s_rows, s_full = slots(3)
    c = copy_section(tabs.at[1], ref["tab_next"], s_tab, after)
    c.start()
    sent.append(c)
    gx = Gather(ref["pay_x"], ref["nx"], ref["xr"], wide)
    later = Gather(ref["pay_l"], ref["nl"], ref["lr"], wide)

    def slot_rows(table, rows):
        picked = [jnp.sum(table[:, c:c + 1] * rows, axis=0, keepdims=True) for c in range(CAP)]
        index = lax.broadcasted_iota(jnp.int32, (CAP, part), 0)
        return jnp.where(index == 0, picked[0], picked[1]).astype(bf16)

    def finish(step, dy, out):
        rf = ref[f"rf{step}"]
        dgate = rf[0, :, part:wide] + rf[4, :, part:wide]
        for q in range(4):
            rows = rf[q, :, 0:part] + rf[q + 4, :, 0:part]
            result = dy(q)
            for c in range(CAP):
                dlog = slopes[step, :, c:c + 1] * dgate[c:c + 1, 0:1]
                row = rows[c:c + 1] + jnp.sum(dlog * router_t[q], axis=0, keepdims=True)
                result = result + tabs[step, :, c:c + 1] * row
            out[q] = result.astype(bf16)

    def one_step(step):
        first_step = step == 0
        local_ref = lambda name: ref[f"{name}{step}"]
        ys = local_ref("yr")
        gy = Gather(ref["pay_y"] if first_step else ref["pay1"], local_ref("ny"), ys, part)
        xs = ref["xr"] if first_step else ref["lr"]
        now = (gx, gy) if first_step else (gy,)
        for g in now:
            g.near_start()
        if first_step:
            later.near_start()
        for g in now:
            g.near_wait()
            g.z_start()
        if first_step:
            later.near_wait()
        for g in now:
            g.z_wait()
        for t in range(2):
            for g in now:
                g.x_start(t)
        if first_step:
            later.z_start()
        else:
            c = copy_section(ref["res0"], ref["inc"], s_full, before)
            c.start()
            sent.append(c)
        for t in range(2):
            for g in now:
                g.x_pass(t)

        pu, ra, sb, rb, dd = (local_ref(name) for name in ("pu", "ra", "sb", "rb", "dd"))
        s1, s2, s3, s4 = slots(2), slots(2), slots(2), slots(2)

        def ends_half(t):
            for g in now:
                g.x_wait(t)
            if not first_step:
                later.x_wait(t)
            pre = jnp.dot(xs[2 * t:2 * t + 2, :, :, 0:part].reshape(128, part), w_in[...], preferred_element_type=f32)
            pu[t, :, :, 0:hidden] = pre.reshape(4, 32, hidden)
            upper = lax.dot_general(
                ys[2 * t:2 * t + 2].reshape(128, part), w_out[...], (((1,), (1,)), ((), ())), preferred_element_type=f32)
            pu[t, :, :, hidden:2 * hidden] = upper.reshape(4, 32, hidden)
            go(pu.at[t, pl.ds(2 * (1 - core), 2)], ra.at[t], s1[t], core_dev)

        for t in range(2):
            ends_half(t)
        if first_step:
            later.z_wait()
            for t in range(2):
                later.x_start(t)
        for t in range(2):
            copy(pu.at[t, pl.ds(2 * (1 - core), 2)], ra.at[t], s1[t], core_dev).wait_recv()
            sb[t] = pu[t, pl.ds(2 * core, 2)] + ra[t]
            go(sb.at[t, 1 - odd], rb.at[t], s2[t], odd_dev)
        k = 2 * core + odd
        for t in range(2):
            copy(sb.at[t, 1 - odd], rb.at[t], s2[t], odd_dev).wait_recv()
            both = sb[t, odd] + rb[t]
            pre = both[:, 0:hidden]
            upper = both[:, hidden:2 * hidden]
            gate = xs[2 * t + core, pl.ds(2 * odd, 2), :, part:wide].reshape(32, EXT).astype(f32)[:, 0:1]
            sig = jax.nn.sigmoid(pre)
            act = pre * sig
            dd[t, k, :, 0:hidden] = (gate * upper * (sig * (1.0 + pre * (1.0 - sig)))).astype(bf16)
            dd[t, k, :, hidden:2 * hidden] = (gate * act).astype(bf16)
            sums = jnp.sum(act * upper, axis=1, keepdims=True)
            dd[t, k, :, 2 * hidden:2 * hidden + EXT] = jnp.broadcast_to(sums, (32, EXT)).astype(bf16)
            go(dd.at[t, k], dd.at[t, k], s3[t], odd_dev)
        if first_step:
            for t in range(2):
                later.x_pass(t)
        for t in range(2):
            copy(dd.at[t, k], dd.at[t, 2 * core + 1 - odd], s3[t], odd_dev).wait_recv()
            pair = dd.at[t, pl.ds(2 * core, 2)]
            go(pair, pair, s4[t], core_dev)

        dx, rx, ry, dz, rz = (local_ref(name) for name in ("dx", "rx", "ry", "dz", "rz"))
        b = [slots(6), slots(6)]

        def piece(t, top, x):
            return dx.at[2 * t + top, x]

        def dx_half(t):
            pair = dd.at[t, pl.ds(2 * core, 2)]
            copy(pair, dd.at[t, pl.ds(2 * (1 - core), 2)], s4[t], core_dev).wait_recv()
            dpre = dd[t, :, :, 0:hidden].reshape(128, hidden)
            term = lax.dot_general(dpre, w_in[...], (((1,), (1,)), ((), ())), preferred_element_type=f32)
            dx[2 * t:2 * t + 2, :, :, 0:part] = term.astype(bf16).reshape(2, 4, 16, part)
            sums = dd[t, :, :, 2 * hidden:2 * hidden + EXT].reshape(128, EXT)
            lanes = lax.broadcasted_iota(jnp.int32, (128, EXT), 1)
            sums = jnp.where(lanes < EXT // 2, sums.astype(f32), 0.0)
            dx[2 * t:2 * t + 2, :, :, part:wide] = sums.astype(bf16).reshape(2, 4, 16, EXT)
            go(piece(t, 0, across), ry.at[t, 0], b[t][0], x_dev(1))
            go(piece(t, 1, across), ry.at[t, 1], b[t][1], x_dev(3))
            go(piece(t, 1, ahead), rx.at[0, 2 * t + 1], b[t][2], x_dev(1))
            go(piece(t, 0, behind), rx.at[1, 2 * t], b[t][3], x_dev(3))

        for t in range(2):
            dx_half(t)
        xmat = xs[:, :, :, 0:part].reshape(256, part)

        ax, az, ah = local_ref("ax"), local_ref("az"), local_ref("ah")
        sums = dd[:, :, :, 2 * hidden:2 * hidden + EXT].reshape(256, EXT)
        pick = (lax.broadcasted_iota(jnp.int32, (16, EXT), 1) == 0).astype(f32).astype(bf16)
        ax[xpos] = lax.dot_general(pick, sums, (((1,), (1,)), ((), ())), preferred_element_type=f32)[0:8]
        sx, sz = slots(3), slots(3)
        sh, = slots(1)
        for r in range(1, 4):
            go(ax.at[xpos], ax.at[xpos], sx[r - 1], x_dev(r))

        dpre = dd[:, :, :, 0:hidden].reshape(256, hidden)
        scaled = dd[:, :, :, hidden:2 * hidden].reshape(256, hidden)

        def joined(first, second):
            value = first.astype(f32) + second.astype(f32)
            column = value[..., part:part + 1] + value[..., part + EXT // 2:part + EXT // 2 + 1]
            return value[..., 0:part].astype(bf16), split_ext(column).astype(bf16)

        def pass_on(t, top, x, device, slot, side):
            z = 2 * t + top
            copy(piece(t, top, x), ry.at[t, top], b[t][top], device).wait_recv()
            main, ext = joined(dx[z, x], ry[t, top])
            dx[z, x, :, 0:part] = main
            dx[z, x, :, part:wide] = ext
            go(piece(t, top, x), rx.at[side, z], b[t][slot], device)

        for t in range(2):
            pass_on(t, 0, ahead, x_dev(1), 4, 0)
            pass_on(t, 1, behind, x_dev(3), 5, 1)
        for r in range(1, 4):
            copy(ax.at[xpos], ax.at[(xpos + 4 - r) % 4], sx[r - 1], x_dev(r)).wait_recv()
        az[zpos] = ax[0] + ax[1] + ax[2] + ax[3]
        for r in range(1, 4):
            go(az.at[zpos], az.at[zpos], sz[r - 1], z_dev(r))
        one = lax.dot_general(xmat, dpre, (((0,), (0,)), ((), ())), preferred_element_type=f32)
        two = lax.dot_general(scaled, ys[...].reshape(256, part), (((0,), (0,)), ((), ())), preferred_element_type=f32)
        if first_step:
            ref["acc_in"][...] = one
            ref["acc_out"][...] = two
        else:
            ref["gin"][...] = (ref["acc_in"][...] + one).astype(bf16)
            ref["gout"][...] = (ref["acc_out"][...] + two).astype(bf16)
        e = slots(3)
        for t in range(2):
            low, high = 2 * t, 2 * t + 1
            copy(piece(t, 1, xpos), rx.at[0, high], b[t][2], x_dev(1)).wait_recv()
            copy(piece(t, 0, xpos), rx.at[1, low], b[t][3], x_dev(3)).wait_recv()
            copy(piece(t, 0, xpos), rx.at[0, low], b[t][4], x_dev(1)).wait_recv()
            copy(piece(t, 1, xpos), rx.at[1, high], b[t][5], x_dev(3)).wait_recv()
            for z in (low, high):
                value = dx[z, xpos].astype(f32) + rx[0, z].astype(f32) + rx[1, z].astype(f32)
                dz[z, :, 0:part] = value[:, 0:part].astype(bf16)
                column = value[:, part:part + 1] + value[:, part + EXT // 2:part + EXT // 2 + 1]
                dz[z, :, part:wide] = split_ext(column).astype(bf16)
            for r in range(1, 4):
                target = (zpos + r) % 4
                c = copy(dz.at[target], rz.at[r - 1], e[r - 1], z_dev(r))
                pl.when(target // 2 == t)(c.start)
                if t == 0:
                    sent.append(c)
        for r in range(1, 4):
            copy(az.at[zpos], az.at[(zpos + 4 - r) % 4], sz[r - 1], z_dev(r)).wait_recv()
        ah[half] = az[0] + az[1] + az[2] + az[3]
        go(ah.at[half], ah.at[half], sh, half_dev)
        copy(ah.at[half], ah.at[1 - half], sh, half_dev).wait_recv()
        dgate = (ah[0] + ah[1])[0:1]
        ext = jnp.transpose(xs[:, :, :, part:wide].reshape(256, EXT).astype(f32))
        slope = ext[8:16] + ext[16:24] + ext[24:32]
        dlog = slope * dgate
        high = rounded(dlog)
        middle = rounded(dlog - high)
        split = jnp.concatenate([high, middle, dlog - high - middle, jnp.zeros_like(high)], axis=0).astype(bf16)
        router = jnp.dot(split, xmat, preferred_element_type=f32)
        router = router[0:8] + router[8:16] + router[16:24]
        if first_step:
            ref["acc_router"][...] = router
        else:
            mine, parts = ref["mine"], ref["parts"]
            mine[...] = ref["acc_router"][...] + router
            held = keep(mine, parts.at[quarter])
            qs = slots(3)
            for r in range(1, 4):
                go(mine, parts.at[quarter], qs[r - 1], base + half * 4 + (quarter + r) % 4)
        for r in range(1, 4):
            copy(dz.at[0], rz.at[r - 1], e[r - 1], z_dev(r)).wait_recv()
        fin, split, rf = local_ref("fin"), local_ref("split"), local_ref("rf")
        value = dz[zpos].astype(f32)
        for r in range(3):
            value = value + rz[r].astype(f32)
        fin[:, 0:part] = value[:, 0:part]
        column = value[:, part:part + 1] + value[:, part + EXT // 2:part + EXT // 2 + 1]
        fin[:, part:wide] = jnp.broadcast_to(column, (16, EXT))
        for s in range(8):
            split[s] = fin[2 * s:2 * s + 2, :]
        stay = keep(split.at[line], rf.at[line])
        n = slots(7)
        for r in range(1, 8):
            go(split.at[(line + r) % 8], rf.at[line], n[r - 1], near_dev(r))
        stay.wait()
        for r in range(1, 8):
            copy(split.at[0], rf.at[(line + 8 - r) % 8], n[r - 1], near_dev(r)).wait_recv()
        if not first_step:
            held.wait()
            for r in range(1, 4):
                copy(mine, parts.at[(quarter + 4 - r) % 4], qs[r - 1], core_dev).wait_recv()
            ref["gr"][...] = parts[...]

    one_step(0)
    res0 = ref["res0"]
    finish(0, lambda q: ref["dy0"][q], res0)
    copy_section(tabs.at[1], ref["tab_next"], s_tab, after).wait_recv()
    for q in range(4):
        ref["rows_out"][q] = slot_rows(ref["tab_next"][...], res0[q].astype(f32))
    c = copy_section(ref["rows_out"], ref["rows_in"], s_rows, before)
    c.start()
    sent.append(c)
    ref["out"][0] = res0[...]
    c.wait_recv()
    for q in range(4):
        own_rows = slot_rows(tabs[1], head[q]).astype(f32)
        ref["pay1"][q] = jnp.where(is_last, own_rows, ref["rows_in"][q].astype(f32)).astype(bf16)
    one_step(1)
    copy_section(res0, ref["inc"], s_full, before).wait_recv()
    live = tabs[1, :, CAP:CAP + 1] > 0.5
    finish(
        1,
        lambda q: jnp.where(live, jnp.where(is_last, head[q], ref["inc"][q].astype(f32)), 0.0),
        ref["out"].at[1],
    )
    for c in sent:
        c.wait_send()


def run_window(experts, sections, ins):
    part, hidden = ins["w_in"].shape
    wide = part + EXT
    bf16, f32 = jnp.bfloat16, jnp.float32
    tokens = ins["dy0"].shape[1]
    outs = {
        "out": ((STEPS, 4, tokens, part), bf16),
        "gin": ((part, hidden), bf16),
        "gout": ((hidden, part), bf16),
        "gr": ((4, experts, part), f32),
    }
    each = {
        "ny": ((8, CAP, part), bf16),
        "yr": ((4, 4, 16, part), bf16),
        "pu": ((2, 4, 32, 2 * hidden), f32),
        "ra": ((2, 2, 32, 2 * hidden), f32),
        "sb": ((2, 2, 32, 2 * hidden), f32),
        "rb": ((2, 32, 2 * hidden), f32),
        "dd": ((2, 4, 32, 2 * hidden + EXT), bf16),
        "dx": ((4, 4, 16, wide), bf16),
        "rx": ((2, 4, 16, wide), bf16),
        "ry": ((2, 2, 16, wide), bf16),
        "dz": ((4, 16, wide), bf16),
        "rz": ((3, 16, wide), bf16),
        "ax": ((4, 8, 256), f32),
        "az": ((4, 8, 256), f32),
        "ah": ((2, 8, 256), f32),
        "fin": ((16, wide), f32),
        "split": ((8, CAP, wide), f32),
        "rf": ((8, CAP, wide), f32),
    }
    scratch = {f"{name}{step}": leaf for step in range(STEPS) for name, leaf in each.items()}
    scratch.update({
        "nx": ((8, CAP, wide), bf16),
        "nl": ((8, CAP, wide), bf16),
        "xr": ((4, 4, 16, wide), bf16),
        "lr": ((4, 4, 16, wide), bf16),
        "acc_in": ((part, hidden), f32),
        "acc_out": ((hidden, part), f32),
        "acc_router": ((experts, part), f32),
        "mine": ((experts, part), f32),
        "parts": ((4, experts, part), f32),
        "tab_next": ((tokens, 128), f32),
        "res0": ((4, tokens, part), bf16),
        "inc": ((4, tokens, part), bf16),
        "rows_out": ((4, CAP, part), bf16),
        "rows_in": ((4, CAP, part), bf16),
        "pay1": ((4, CAP, part), bf16),
    })
    names = list(ins) + list(outs) + list(scratch) + ["send", "recv", "own"]
    vmem = pl.BlockSpec(memory_space=pltpu.VMEM)
    copies = 240
    got = pl.pallas_call(
        functools.partial(window_kernel, part, hidden, experts, sections, names),
        out_shape=[jax.ShapeDtypeStruct(*leaf) for leaf in outs.values()],
        in_specs=[vmem] * len(ins),
        out_specs=[vmem] * len(outs),
        scratch_shapes=[pltpu.VMEM(*leaf) for leaf in scratch.values()]
        + [pltpu.SemaphoreType.DMA((copies,)), pltpu.SemaphoreType.DMA((copies,)), pltpu.SemaphoreType.DMA((8,))],
        compiler_params=pltpu.CompilerParams(
            collective_id=0, has_side_effects=True, vmem_limit_bytes=48 << 20
        ),
    )(*ins.values())
    return dict(zip(outs, got))


def local(saved_inputs, carried, head_grad, routing, replica_counts, router, w_in, w_out):
    hi = lax.Precision.HIGHEST
    section_index = lax.axis_index("section")
    dev_index = lax.axis_index("dp")
    width = head_grad.shape[1]
    part = w_in.shape[2]
    experts = router.shape[2]
    router_w = router[0]
    my_count = replica_counts[dev_index]
    first = (jnp.arange(experts) == 0).astype(jnp.float32)
    slots = jnp.arange(CAP, dtype=jnp.int32)

    def quarters(rows):
        return rows.reshape(CAP, 4, part).transpose(1, 0, 2)

    def prepare(step):
        xin = saved_inputs[0, step]
        ids = routing[0, step]
        live = step + section_index < my_count
        xf = xin.astype(jnp.float32)
        logits = jnp.dot(xf, router_w, precision=hi)
        expo = jnp.exp(logits)
        prob = expo / jnp.sum(expo, axis=1, keepdims=True)
        routed = ((ids[:, 0] == 0) | (ids[:, 1] == 0)) & live
        slot = jnp.cumsum(routed.astype(jnp.int32), dtype=jnp.int32) - 1
        table = ((slot[None, :] == slots[:, None]) & routed[None, :]).astype(jnp.float32)
        xs = jnp.dot(table.astype(jnp.bfloat16), xin, preferred_element_type=jnp.float32).astype(jnp.bfloat16)
        gate = jnp.dot(table, prob[:, 0], precision=hi).astype(jnp.bfloat16)
        slope = jnp.dot(table, prob[:, :1] * (first[None, :] - prob), precision=hi)
        high = rounded(slope)
        middle = rounded(slope - high)
        low = rounded(slope - high - middle)
        ext = jnp.concatenate(
            [jnp.broadcast_to(gate.astype(jnp.float32)[:, None], (CAP, 8)), high, middle, low], axis=1)
        ext = jnp.pad(ext, ((0, 0), (0, EXT - ext.shape[1]))).astype(jnp.bfloat16)
        payload = jnp.concatenate([quarters(xs), jnp.broadcast_to(ext[None], (4, CAP, EXT))], axis=2)
        column = jnp.concatenate([table.T, live.astype(jnp.float32) * jnp.ones((xin.shape[0], 1))], axis=1)
        column = jnp.pad(column, ((0, 0), (0, 128 - column.shape[1])))
        return (table, live, payload, column, jnp.pad(slope.T, ((0, 0), (0, 128 - CAP))))

    prepared = [prepare(step) for step in range(STEPS)]
    def token_quarters(rows):
        return rows.astype(jnp.float32).reshape(-1, 4, part).transpose(1, 0, 2)

    table, live, payload, *_ = prepared[0]
    dy = jnp.where(live, carried[0], jnp.zeros_like(carried[0]))
    ys = jnp.dot(table.astype(jnp.bfloat16), dy, preferred_element_type=jnp.float32).astype(jnp.bfloat16)
    got = run_window(experts, lax.axis_size("section"), {
        "w_in": w_in[0, 0],
        "w_out": w_out[0, 0],
        "pay_y": quarters(ys),
        "pay_x": payload,
        "pay_l": prepared[1][2],
        "dy0": token_quarters(dy),
        "head": token_quarters(head_grad),
        "tabs": jnp.stack([prepared[step][3] for step in range(STEPS)]),
        "slopes": jnp.stack([prepared[step][4] for step in range(STEPS)]),
        "router_t": router_w.T.reshape(experts, 4, part).transpose(1, 0, 2),
    })
    grad_router = got["gr"].transpose(0, 2, 1).reshape(width, experts)
    input_grad = got["out"].transpose(0, 2, 1, 3).reshape(STEPS, 1, -1, width)
    return (input_grad, got["gin"][None, None], got["gout"][None, None], grad_router[None])


def solution(mesh):
    in_specs = (
        P("section", None, "dp", None),
        P("section", "dp", None),
        P("dp", None),
        P("section", None, "dp", None),
        P(),
        P("section", None, None),
        P("section", "dp", None, None),
        P("section", "dp", None, None),
    )
    out_specs = (
        P(None, "section", "dp", None),
        P("section", "dp", None, None),
        P("section", "dp", None, None),
        P("section", None, None),
    )
    return jax.shard_map(local, mesh=mesh, in_specs=in_specs, out_specs=out_specs, check_vma=False)
```

```python
import functools

import jax
import jax.numpy as jnp
from jax import lax
from jax.experimental import pallas as pl
from jax.experimental.pallas import tpu as pltpu
from jax.sharding import PartitionSpec as P

STEPS = 2
CAP = 2
EXT = 128


def rounded(value):
    return value.astype(jnp.bfloat16).astype(jnp.float32)


def split_ext(value):
    lanes = lax.broadcasted_iota(jnp.int32, value.shape[:-1] + (EXT,), len(value.shape) - 1)
    high = rounded(value)
    return jnp.where(lanes < EXT // 2, high, value - high)


def window_kernel(part, hidden, experts, sections, names, *refs):
    ref = dict(zip(names, refs))
    w_in, w_out = ref["w_in"], ref["w_out"]
    send, recv, own = ref["send"], ref["recv"], ref["own"]
    wide = part + EXT
    f32, bf16 = jnp.float32, jnp.bfloat16
    me = lax.axis_index("dp")
    section = lax.axis_index("section")
    before, after = (section + sections - 1) % sections, (section + 1) % sections
    line = me % 8
    base = me - line
    core = me % 2
    odd = (me // 2) % 2
    half = line // 4
    quarter = me % 4
    xpos = (me // 8) % 4
    zpos = me // 32
    ahead, behind, across = (xpos + 1) % 4, (xpos + 3) % 4, (xpos + 2) % 4

    def near_dev(r):
        return base + (line + r) % 8

    def z_dev(r):
        return ((zpos + r) % 4) * 32 + xpos * 8 + line

    def x_dev(r):
        return zpos * 32 + ((xpos + r) % 4) * 8 + line

    core_dev = base + (line // 2) * 2 + (1 - core)
    odd_dev = base + half * 4 + (1 - odd) * 2 + core
    half_dev = base + (line + 4) % 8

    barrier = pltpu.get_barrier_semaphore()
    peers = [near_dev(r) for r in range(1, 8)]
    peers += [z_dev(r) for r in range(1, 4)] + [x_dev(r) for r in range(1, 4)]
    for peer in peers:
        pl.semaphore_signal(barrier, inc=1, device_id={"dp": peer}, device_id_type=pl.DeviceIdType.MESH)
    for neighbour in (before, after):
        pl.semaphore_signal(
            barrier, inc=1, device_id={"section": neighbour}, device_id_type=pl.DeviceIdType.MESH)
    pl.semaphore_wait(barrier, len(peers) + 2)

    def copy(src, dst, slot, device):
        return pltpu.make_async_remote_copy(
            src_ref=src, dst_ref=dst, send_sem=send.at[slot], recv_sem=recv.at[slot],
            device_id={"dp": device}, device_id_type=pl.DeviceIdType.MESH)

    def copy_section(src, dst, slot, target):
        return pltpu.make_async_remote_copy(
            src_ref=src, dst_ref=dst, send_sem=send.at[slot], recv_sem=recv.at[slot],
            device_id={"section": target}, device_id_type=pl.DeviceIdType.MESH)

    sent, taken, kept = [], [0], [0]

    def slots(count):
        taken[0] += count
        return list(range(taken[0] - count, taken[0]))

    def go(src, dst, slot, device):
        c = copy(src, dst, slot, device)
        c.start()
        sent.append(c)

    def keep(src, dst):
        c = pltpu.make_async_copy(src, dst, own.at[kept[0]])
        kept[0] += 1
        c.start()
        return c

    class Gather:
        def __init__(self, pay, near, rows, columns):
            self.pay, self.near, self.rows, self.columns = pay, near, rows, columns
            self.n, self.z, self.x = slots(7), slots(3), slots(6)

        def near_start(self):
            self.mine = keep(self.pay.at[quarter], self.near.at[line])
            for r in range(1, 8):
                go(self.pay.at[(line + r) % 4], self.near.at[line], self.n[r - 1], near_dev(r))

        def near_wait(self):
            self.mine.wait()
            for r in range(1, 8):
                copy(self.pay.at[0], self.near.at[(line + 8 - r) % 8], self.n[r - 1], near_dev(r)).wait_recv()
            for at in range(0, self.columns, 512):
                size = min(512, self.columns - at)
                index = lax.broadcasted_iota(jnp.int32, (16, size), 0)
                block = jnp.zeros((16, size), f32)
                for s in range(8):
                    pair = self.near[s, :, at:at + size].astype(f32)
                    for k in range(2):
                        block = jnp.where(index == 2 * s + k, pair[k:k + 1], block)
                self.rows[zpos, xpos, :, at:at + size] = block.astype(bf16)

        def z_start(self):
            for r in range(1, 4):
                go(self.rows.at[zpos, xpos], self.rows.at[zpos, xpos], self.z[r - 1], z_dev(r))

        def z_wait(self):
            for r in range(1, 4):
                copy(self.rows.at[zpos, xpos], self.rows.at[(zpos + 4 - r) % 4, xpos], self.z[r - 1], z_dev(r)).wait_recv()

        def piece(self, top, x):
            return self.rows.at[pl.ds(2 * top, 2), x]

        def x_start(self):
            go(self.piece(0, xpos), self.piece(0, xpos), self.x[0], x_dev(1))
            go(self.piece(1, xpos), self.piece(1, xpos), self.x[1], x_dev(3))
            go(self.piece(1, xpos), self.piece(1, xpos), self.x[2], x_dev(1))
            go(self.piece(0, xpos), self.piece(0, xpos), self.x[3], x_dev(3))

        def x_pass(self):
            copy(self.piece(0, xpos), self.piece(0, behind), self.x[0], x_dev(1)).wait_recv()
            go(self.piece(0, behind), self.piece(0, behind), self.x[4], x_dev(1))
            copy(self.piece(1, xpos), self.piece(1, ahead), self.x[1], x_dev(3)).wait_recv()
            go(self.piece(1, ahead), self.piece(1, ahead), self.x[5], x_dev(3))

        def x_wait(self):
            copy(self.piece(1, xpos), self.piece(1, behind), self.x[2], x_dev(1)).wait_recv()
            copy(self.piece(0, xpos), self.piece(0, ahead), self.x[3], x_dev(3)).wait_recv()
            copy(self.piece(0, xpos), self.piece(0, across), self.x[4], x_dev(1)).wait_recv()
            copy(self.piece(1, xpos), self.piece(1, across), self.x[5], x_dev(3)).wait_recv()

    tabs, slopes, router_t, head = ref["tabs"], ref["slopes"], ref["router_t"], ref["head"]
    is_last = section == sections - 1
    s_tab, s_rows, s_full = slots(3)
    c = copy_section(tabs.at[1], ref["tab_next"], s_tab, after)
    c.start()
    sent.append(c)
    gx = Gather(ref["pay_x"], ref["nx"], ref["xr"], wide)
    later = Gather(ref["pay_l"], ref["nl"], ref["lr"], wide)

    def slot_rows(table, rows):
        picked = [jnp.sum(table[:, c:c + 1] * rows, axis=0, keepdims=True) for c in range(CAP)]
        index = lax.broadcasted_iota(jnp.int32, (CAP, part), 0)
        return jnp.where(index == 0, picked[0], picked[1]).astype(bf16)

    def finish(step, dy, out):
        rf = ref[f"rf{step}"]
        dgate = rf[0, :, part:wide] + rf[4, :, part:wide]
        for q in range(4):
            rows = rf[q, :, 0:part] + rf[q + 4, :, 0:part]
            result = dy(q)
            for c in range(CAP):
                dlog = slopes[step, :, c:c + 1] * dgate[c:c + 1, 0:1]
                row = rows[c:c + 1] + jnp.sum(dlog * router_t[q], axis=0, keepdims=True)
                result = result + tabs[step, :, c:c + 1] * row
            out[q] = result.astype(bf16)

    def one_step(step):
        first_step = step == 0
        local_ref = lambda name: ref[f"{name}{step}"]
        ys = local_ref("yr")
        gy = Gather(ref["pay_y"] if first_step else ref["pay1"], local_ref("ny"), ys, part)
        xs = ref["xr"] if first_step else ref["lr"]
        now = (gx, gy) if first_step else (gy,)
        for g in now:
            g.near_start()
        if first_step:
            later.near_start()
        for g in now:
            g.near_wait()
            g.z_start()
        if first_step:
            later.near_wait()
        for g in now:
            g.z_wait()
            g.x_start()
        if first_step:
            later.z_start()
        else:
            c = copy_section(ref["res0"], ref["inc"], s_full, before)
            c.start()
            sent.append(c)
        for g in now:
            g.x_pass()
        for g in now:
            g.x_wait()

        if not first_step:
            later.x_wait()
        xmat = xs[:, :, :, 0:part].reshape(256, part)
        pu, ra, sb, rb, dd = local_ref("pu"), local_ref("ra"), local_ref("sb"), local_ref("rb"), local_ref("dd")
        pre = jnp.dot(xmat, w_in[...], preferred_element_type=f32)
        pu[:, :, 0:hidden] = pre.reshape(4, 64, hidden)
        upper = lax.dot_general(ys[...].reshape(256, part), w_out[...], (((1,), (1,)), ((), ())), preferred_element_type=f32)
        pu[:, :, hidden:2 * hidden] = upper.reshape(4, 64, hidden)

        s1, s2, s3, s4 = slots(4)
        go(pu.at[pl.ds(2 * (1 - core), 2)], ra, s1, core_dev)
        copy(pu.at[pl.ds(2 * (1 - core), 2)], ra, s1, core_dev).wait_recv()
        sb[...] = pu[pl.ds(2 * core, 2)] + ra[...]
        go(sb.at[1 - odd], rb, s2, odd_dev)
        copy(sb.at[1 - odd], rb, s2, odd_dev).wait_recv()
        k = 2 * core + odd
        both = sb[odd] + rb[...]
        pre = both[:, 0:hidden]
        upper = both[:, hidden:2 * hidden]
        gate = xs[k, :, :, part:wide].reshape(64, EXT).astype(f32)[:, 0:1]
        sig = jax.nn.sigmoid(pre)
        act = pre * sig
        dd[k, :, 0:hidden] = (gate * upper * (sig * (1.0 + pre * (1.0 - sig)))).astype(bf16)
        dd[k, :, hidden:2 * hidden] = (gate * act).astype(bf16)
        sums = jnp.sum(act * upper, axis=1, keepdims=True)
        dd[k, :, 2 * hidden:2 * hidden + EXT] = jnp.broadcast_to(sums, (64, EXT)).astype(bf16)
        go(dd.at[k], dd.at[k], s3, odd_dev)
        copy(dd.at[k], dd.at[2 * core + 1 - odd], s3, odd_dev).wait_recv()
        go(dd.at[pl.ds(2 * core, 2)], dd.at[pl.ds(2 * core, 2)], s4, core_dev)
        copy(dd.at[pl.ds(2 * core, 2)], dd.at[pl.ds(2 * (1 - core), 2)], s4, core_dev).wait_recv()

        ax, az, ah = local_ref("ax"), local_ref("az"), local_ref("ah")
        sums = dd[:, :, 2 * hidden:2 * hidden + EXT].reshape(256, EXT)
        pick = (lax.broadcasted_iota(jnp.int32, (16, EXT), 1) == 0).astype(f32).astype(bf16)
        ax[xpos] = lax.dot_general(pick, sums, (((1,), (1,)), ((), ())), preferred_element_type=f32)[0:8]
        sx, sz = slots(3), slots(3)
        sh, = slots(1)
        for r in range(1, 4):
            go(ax.at[xpos], ax.at[xpos], sx[r - 1], x_dev(r))

        dx, rx, ry, dz, rz = local_ref("dx"), local_ref("rx"), local_ref("ry"), local_ref("dz"), local_ref("rz")
        dpre = dd[:, :, 0:hidden].reshape(256, hidden)
        scaled = dd[:, :, hidden:2 * hidden].reshape(256, hidden)
        term = lax.dot_general(dpre, w_in[...], (((1,), (1,)), ((), ())), preferred_element_type=f32)
        dx[:, :, :, 0:part] = term.astype(bf16).reshape(4, 4, 16, part)
        lanes = lax.broadcasted_iota(jnp.int32, (256, EXT), 1)
        sums = jnp.where(lanes < EXT // 2, sums.astype(f32), 0.0)
        dx[:, :, :, part:wide] = sums.astype(bf16).reshape(4, 4, 16, EXT)

        def piece(top, x):
            return dx.at[pl.ds(2 * top, 2), x]

        b = slots(6)
        go(piece(0, across), ry.at[0], b[0], x_dev(1))
        go(piece(1, across), ry.at[1], b[1], x_dev(3))
        go(piece(1, ahead), rx.at[0, pl.ds(2, 2)], b[2], x_dev(1))
        go(piece(0, behind), rx.at[1, pl.ds(0, 2)], b[3], x_dev(3))
        for r in range(1, 4):
            copy(ax.at[xpos], ax.at[(xpos + 4 - r) % 4], sx[r - 1], x_dev(r)).wait_recv()
        az[zpos] = ax[0] + ax[1] + ax[2] + ax[3]
        for r in range(1, 4):
            go(az.at[zpos], az.at[zpos], sz[r - 1], z_dev(r))

        def joined(first, second):
            value = first.astype(f32) + second.astype(f32)
            column = value[..., part:part + 1] + value[..., part + EXT // 2:part + EXT // 2 + 1]
            return value[..., 0:part].astype(bf16), split_ext(column).astype(bf16)

        def pass_on(top, x, slot, came, device):
            copy(piece(top, x), ry.at[came], slot, device).wait_recv()
            for z in range(2):
                main, ext = joined(dx[2 * top + z, x], ry[came, z])
                dx[2 * top + z, x, :, 0:part] = main
                dx[2 * top + z, x, :, part:wide] = ext

        pass_on(0, ahead, b[0], 0, x_dev(1))
        go(piece(0, ahead), rx.at[0, pl.ds(0, 2)], b[4], x_dev(1))
        pass_on(1, behind, b[1], 1, x_dev(3))
        go(piece(1, behind), rx.at[1, pl.ds(2, 2)], b[5], x_dev(3))
        one = lax.dot_general(xmat, dpre, (((0,), (0,)), ((), ())), preferred_element_type=f32)
        two = lax.dot_general(scaled, ys[...].reshape(256, part), (((0,), (0,)), ((), ())), preferred_element_type=f32)
        if first_step:
            ref["acc_in"][...] = one
            ref["acc_out"][...] = two
        else:
            ref["gin"][...] = (ref["acc_in"][...] + one).astype(bf16)
            ref["gout"][...] = (ref["acc_out"][...] + two).astype(bf16)
        for r in range(1, 4):
            copy(az.at[zpos], az.at[(zpos + 4 - r) % 4], sz[r - 1], z_dev(r)).wait_recv()
        ah[half] = az[0] + az[1] + az[2] + az[3]
        go(ah.at[half], ah.at[half], sh, half_dev)
        copy(piece(1, xpos), rx.at[0, pl.ds(2, 2)], b[2], x_dev(1)).wait_recv()
        copy(piece(0, xpos), rx.at[1, pl.ds(0, 2)], b[3], x_dev(3)).wait_recv()
        copy(piece(0, xpos), rx.at[0, pl.ds(0, 2)], b[4], x_dev(1)).wait_recv()
        copy(piece(1, xpos), rx.at[1, pl.ds(2, 2)], b[5], x_dev(3)).wait_recv()
        for z in range(4):
            value = dx[z, xpos].astype(f32) + rx[0, z].astype(f32) + rx[1, z].astype(f32)
            dz[z, :, 0:part] = value[:, 0:part].astype(bf16)
            column = value[:, part:part + 1] + value[:, part + EXT // 2:part + EXT // 2 + 1]
            dz[z, :, part:wide] = split_ext(column).astype(bf16)
        e = slots(3)
        for r in range(1, 4):
            go(dz.at[(zpos + r) % 4], rz.at[r - 1], e[r - 1], z_dev(r))
        if first_step:
            later.z_wait()
            later.x_start()
        copy(ah.at[half], ah.at[1 - half], sh, half_dev).wait_recv()
        dgate = (ah[0] + ah[1])[0:1]
        ext = jnp.transpose(xs[:, :, :, part:wide].reshape(256, EXT).astype(f32))
        slope = ext[8:16] + ext[16:24] + ext[24:32]
        dlog = slope * dgate
        high = rounded(dlog)
        middle = rounded(dlog - high)
        split = jnp.concatenate([high, middle, dlog - high - middle, jnp.zeros_like(high)], axis=0).astype(bf16)
        router = jnp.dot(split, xmat, preferred_element_type=f32)
        router = router[0:8] + router[8:16] + router[16:24]
        if first_step:
            ref["acc_router"][...] = router
        else:
            mine, parts = ref["mine"], ref["parts"]
            mine[...] = ref["acc_router"][...] + router
            held = keep(mine, parts.at[quarter])
            qs = slots(3)
            for r in range(1, 4):
                go(mine, parts.at[quarter], qs[r - 1], base + half * 4 + (quarter + r) % 4)
        for r in range(1, 4):
            copy(dz.at[0], rz.at[r - 1], e[r - 1], z_dev(r)).wait_recv()
        fin, split, rf = local_ref("fin"), local_ref("split"), local_ref("rf")
        value = dz[zpos].astype(f32)
        for r in range(3):
            value = value + rz[r].astype(f32)
        fin[:, 0:part] = value[:, 0:part]
        column = value[:, part:part + 1] + value[:, part + EXT // 2:part + EXT // 2 + 1]
        fin[:, part:wide] = jnp.broadcast_to(column, (16, EXT))
        for s in range(8):
            split[s] = fin[2 * s:2 * s + 2, :]
        stay = keep(split.at[line], rf.at[line])
        n = slots(7)
        for r in range(1, 8):
            go(split.at[(line + r) % 8], rf.at[line], n[r - 1], near_dev(r))
        if first_step:
            later.x_pass()
        stay.wait()
        for r in range(1, 8):
            copy(split.at[0], rf.at[(line + 8 - r) % 8], n[r - 1], near_dev(r)).wait_recv()
        if not first_step:
            held.wait()
            for r in range(1, 4):
                copy(mine, parts.at[(quarter + 4 - r) % 4], qs[r - 1], core_dev).wait_recv()
            ref["gr"][...] = parts[...]

    one_step(0)
    res0 = ref["res0"]
    finish(0, lambda q: ref["dy0"][q], res0)
    copy_section(tabs.at[1], ref["tab_next"], s_tab, after).wait_recv()
    for q in range(4):
        ref["rows_out"][q] = slot_rows(ref["tab_next"][...], res0[q].astype(f32))
    c = copy_section(ref["rows_out"], ref["rows_in"], s_rows, before)
    c.start()
    sent.append(c)
    ref["out"][0] = res0[...]
    c.wait_recv()
    for q in range(4):
        own_rows = slot_rows(tabs[1], head[q]).astype(f32)
        ref["pay1"][q] = jnp.where(is_last, own_rows, ref["rows_in"][q].astype(f32)).astype(bf16)
    one_step(1)
    copy_section(res0, ref["inc"], s_full, before).wait_recv()
    live = tabs[1, :, CAP:CAP + 1] > 0.5
    finish(
        1,
        lambda q: jnp.where(live, jnp.where(is_last, head[q], ref["inc"][q].astype(f32)), 0.0),
        ref["out"].at[1],
    )
    for c in sent:
        c.wait_send()


def run_window(experts, sections, ins):
    part, hidden = ins["w_in"].shape
    wide = part + EXT
    bf16, f32 = jnp.bfloat16, jnp.float32
    tokens = ins["dy0"].shape[1]
    outs = {
        "out": ((STEPS, 4, tokens, part), bf16),
        "gin": ((part, hidden), bf16),
        "gout": ((hidden, part), bf16),
        "gr": ((4, experts, part), f32),
    }
    each = {
        "ny": ((8, CAP, part), bf16),
        "yr": ((4, 4, 16, part), bf16),
        "pu": ((4, 64, 2 * hidden), f32),
        "ra": ((2, 64, 2 * hidden), f32),
        "sb": ((2, 64, 2 * hidden), f32),
        "rb": ((64, 2 * hidden), f32),
        "dd": ((4, 64, 2 * hidden + EXT), bf16),
        "dx": ((4, 4, 16, wide), bf16),
        "rx": ((2, 4, 16, wide), bf16),
        "ry": ((2, 2, 16, wide), bf16),
        "dz": ((4, 16, wide), bf16),
        "rz": ((3, 16, wide), bf16),
        "ax": ((4, 8, 256), f32),
        "az": ((4, 8, 256), f32),
        "ah": ((2, 8, 256), f32),
        "fin": ((16, wide), f32),
        "split": ((8, CAP, wide), f32),
        "rf": ((8, CAP, wide), f32),
    }
    scratch = {f"{name}{step}": leaf for step in range(STEPS) for name, leaf in each.items()}
    scratch.update({
        "nx": ((8, CAP, wide), bf16),
        "nl": ((8, CAP, wide), bf16),
        "xr": ((4, 4, 16, wide), bf16),
        "lr": ((4, 4, 16, wide), bf16),
        "acc_in": ((part, hidden), f32),
        "acc_out": ((hidden, part), f32),
        "acc_router": ((experts, part), f32),
        "mine": ((experts, part), f32),
        "parts": ((4, experts, part), f32),
        "tab_next": ((tokens, 128), f32),
        "res0": ((4, tokens, part), bf16),
        "inc": ((4, tokens, part), bf16),
        "rows_out": ((4, CAP, part), bf16),
        "rows_in": ((4, CAP, part), bf16),
        "pay1": ((4, CAP, part), bf16),
    })
    names = list(ins) + list(outs) + list(scratch) + ["send", "recv", "own"]
    vmem = pl.BlockSpec(memory_space=pltpu.VMEM)
    copies = 160
    got = pl.pallas_call(
        functools.partial(window_kernel, part, hidden, experts, sections, names),
        out_shape=[jax.ShapeDtypeStruct(*leaf) for leaf in outs.values()],
        in_specs=[vmem] * len(ins),
        out_specs=[vmem] * len(outs),
        scratch_shapes=[pltpu.VMEM(*leaf) for leaf in scratch.values()]
        + [pltpu.SemaphoreType.DMA((copies,)), pltpu.SemaphoreType.DMA((copies,)), pltpu.SemaphoreType.DMA((8,))],
        compiler_params=pltpu.CompilerParams(
            collective_id=0, has_side_effects=True, vmem_limit_bytes=48 << 20
        ),
    )(*ins.values())
    return dict(zip(outs, got))


def local(saved_inputs, carried, head_grad, routing, replica_counts, router, w_in, w_out):
    hi = lax.Precision.HIGHEST
    section_index = lax.axis_index("section")
    dev_index = lax.axis_index("dp")
    width = head_grad.shape[1]
    part = w_in.shape[2]
    experts = router.shape[2]
    router_w = router[0]
    my_count = replica_counts[dev_index]
    first = (jnp.arange(experts) == 0).astype(jnp.float32)
    slots = jnp.arange(CAP, dtype=jnp.int32)

    def quarters(rows):
        return rows.reshape(CAP, 4, part).transpose(1, 0, 2)

    def prepare(step):
        xin = saved_inputs[0, step]
        ids = routing[0, step]
        live = step + section_index < my_count
        xf = xin.astype(jnp.float32)
        logits = jnp.dot(xf, router_w, precision=hi)
        expo = jnp.exp(logits)
        prob = expo / jnp.sum(expo, axis=1, keepdims=True)
        routed = ((ids[:, 0] == 0) | (ids[:, 1] == 0)) & live
        slot = jnp.cumsum(routed.astype(jnp.int32), dtype=jnp.int32) - 1
        table = ((slot[None, :] == slots[:, None]) & routed[None, :]).astype(jnp.float32)
        xs = jnp.dot(table.astype(jnp.bfloat16), xin, preferred_element_type=jnp.float32).astype(jnp.bfloat16)
        gate = jnp.dot(table, prob[:, 0], precision=hi).astype(jnp.bfloat16)
        slope = jnp.dot(table, prob[:, :1] * (first[None, :] - prob), precision=hi)
        high = rounded(slope)
        middle = rounded(slope - high)
        low = rounded(slope - high - middle)
        ext = jnp.concatenate(
            [jnp.broadcast_to(gate.astype(jnp.float32)[:, None], (CAP, 8)), high, middle, low], axis=1)
        ext = jnp.pad(ext, ((0, 0), (0, EXT - ext.shape[1]))).astype(jnp.bfloat16)
        payload = jnp.concatenate([quarters(xs), jnp.broadcast_to(ext[None], (4, CAP, EXT))], axis=2)
        column = jnp.concatenate([table.T, live.astype(jnp.float32) * jnp.ones((xin.shape[0], 1))], axis=1)
        column = jnp.pad(column, ((0, 0), (0, 128 - column.shape[1])))
        return (table, live, payload, column, jnp.pad(slope.T, ((0, 0), (0, 128 - CAP))))

    prepared = [prepare(step) for step in range(STEPS)]
    def token_quarters(rows):
        return rows.astype(jnp.float32).reshape(-1, 4, part).transpose(1, 0, 2)

    table, live, payload, *_ = prepared[0]
    dy = jnp.where(live, carried[0], jnp.zeros_like(carried[0]))
    ys = jnp.dot(table.astype(jnp.bfloat16), dy, preferred_element_type=jnp.float32).astype(jnp.bfloat16)
    got = run_window(experts, lax.axis_size("section"), {
        "w_in": w_in[0, 0],
        "w_out": w_out[0, 0],
        "pay_y": quarters(ys),
        "pay_x": payload,
        "pay_l": prepared[1][2],
        "dy0": token_quarters(dy),
        "head": token_quarters(head_grad),
        "tabs": jnp.stack([prepared[step][3] for step in range(STEPS)]),
        "slopes": jnp.stack([prepared[step][4] for step in range(STEPS)]),
        "router_t": router_w.T.reshape(experts, 4, part).transpose(1, 0, 2),
    })
    grad_router = got["gr"].transpose(0, 2, 1).reshape(width, experts)
    input_grad = got["out"].transpose(0, 2, 1, 3).reshape(STEPS, 1, -1, width)
    return (input_grad, got["gin"][None, None], got["gout"][None, None], grad_router[None])


def solution(mesh):
    in_specs = (
        P("section", None, "dp", None),
        P("section", "dp", None),
        P("dp", None),
        P("section", None, "dp", None),
        P(),
        P("section", None, None),
        P("section", "dp", None, None),
        P("section", "dp", None, None),
    )
    out_specs = (
        P(None, "section", "dp", None),
        P("section", "dp", None, None),
        P("section", "dp", None, None),
        P("section", None, None),
    )
    return jax.shard_map(local, mesh=mesh, in_specs=in_specs, out_specs=out_specs, check_vma=False)
```
